128 devices in a mesh: row: 8 (over z, x_hi), col: 16 (over y, x_lo, core).
Axes of the slice: x: 4 (x_hi: 2, x_lo: 2; x = x_hi * 2 + x_lo), y: 4, z: 4, core: 2. Of those that a mesh axis runs over, the one named last changes fastest.
Arguments:
- interaction: bfloat16 [12288, 6144], P('row', 'col'), may hold values from -0.078125 to 0.078125
- cycle_amps: bfloat16 [6144, 12288], P('row', 'col'), may hold values from -6 to 6
- tile_mask: int32 [16, 8], replicated, may hold values 0 or 1
- virt_perm: int32 [384], replicated, may hold values from 0 to 383, each once
- occ_energy: float32 [32], replicated, may hold values from -2 to -0.5
- virt_energy: float32 [384], replicated, may hold values from 0.2 to 3
- old_amps: bfloat16 [12288, 12288], P(('row', 'col')), may hold values from -6 to 6
Outputs:
- new_amps: float32 [12288, 12288], P(('row', 'col'))
The draws below stay inside these ranges and needn't reach their ends.
Inputs may be any that keep to these rules, and one draw needn't show every extreme that they name: `tile_mask`: 0 or 1 for each tile. `virt_perm`: each number of 0 to 383 once.
All inputs are finite; a program needn't handle non-finite values.
Results may differ from the reference program's by a relative error of at most 0.0012.
Values may be sent and summed in bfloat16 or wider, within the bound.
A program may use at most 320 MiB of HBM per device.

```python
import jax
import jax.numpy as jnp

O = 32
V = 384
TILE = 768
K = 6144
M = 12288
MT = 16
KT = 8


def touch_ends(result, stream_key, smallest, high):
    longest = result.shape.index(max(result.shape))
    spots = []
    for shift in (0, 1):
        where = [jax.random.randint(jax.random.fold_in(stream_key, axis), (), 0, length) for axis, length in enumerate(result.shape)]
        where[longest] = (where[longest] + shift) % result.shape[longest]
        spots.append(tuple(where))
    return result.at[spots[0]].set(smallest).at[spots[1]].set(high)


def steps_of(rng, extent, split, low, largest):
    gain = 1.0
    for position, shards_of in split:
        steps = jax.random.uniform(jax.random.fold_in(jax.random.fold_in(rng, 6), position), (shards_of,), jnp.float32, low / len(split), largest / len(split))
        gain = gain * jnp.repeat(jnp.exp(steps), extent[position] // shards_of).reshape((-1,) + (1,) * (len(extent) - 1 - position))
    return gain


def bell_draw(key, shape, deviation, reach, pieces=(), held_as=jnp.bfloat16):
    drawn = deviation * jax.random.normal(key, shape, jnp.float32)
    if pieces:
        drawn = drawn * steps_of(key, shape, pieces, -0.22, 0.18)
    return jnp.clip(drawn, -reach, reach).astype(held_as)


def setup_inputs(seed: int = 0) -> dict:
    streams_of = jax.random.split(jax.random.key(seed), 8)
    return {
        "interaction": bell_draw(streams_of[0], (M, K), K ** -0.5, 0.078125, ((0, 8), (1, 16))),
        "cycle_amps": bell_draw(streams_of[1], (K, M), 1.0, 6.0, ((0, 8), (1, 16))),
        "tile_mask": touch_ends((jax.random.randint(streams_of[2], (MT, KT), 0, 2) < 1).astype(jnp.int32), jax.random.fold_in(streams_of[2], 1), 0, 1),
        "virt_perm": jax.random.permutation(streams_of[3], V).astype(jnp.int32),
        "occ_energy": jnp.clip(jax.random.uniform(streams_of[4], (O,), jnp.float32, -2.0, -0.5), -2.0, -0.5),
        "virt_energy": jnp.clip(jax.random.uniform(streams_of[5], (V,), jnp.float32, 0.2, 3.0), 0.2, 3.0),
        "old_amps": bell_draw(streams_of[6], (M, M), 1.0, 6.0, ((0, 128),)),
    }


def reference(interaction, cycle_amps, tile_mask, virt_perm, occ_energy, virt_energy, old_amps):
    mask_full = jnp.repeat(jnp.repeat(tile_mask, TILE, axis=0), TILE, axis=1).astype(jnp.bfloat16)
    masked = interaction * mask_full
    cycle_term = jnp.dot(masked, cycle_amps, preferred_element_type=jnp.float32)
    grid = cycle_term.reshape(O, V, O, V)
    permuted = jnp.take(jnp.take(grid, virt_perm, axis=1), virt_perm, axis=3)
    exchange_term = jnp.transpose(permuted, (0, 3, 2, 1)).reshape(M, M)
    combined = (2.0 * cycle_term - exchange_term).astype(jnp.bfloat16)
    paired = combined.astype(jnp.float32) + combined.T.astype(jnp.float32)
    pair_energy = (virt_energy[None, :] - occ_energy[:, None]).reshape(M)
    denominator = pair_energy[:, None] + pair_energy[None, :]
    return old_amps.astype(jnp.float32) + paired / denominator
```

```python
import functools

import jax
import jax.numpy as jnp
from jax import lax
from jax.experimental import pallas as pl
from jax.experimental.pallas import tpu as pltpu
from jax.sharding import PartitionSpec as P

V = 384
TILE = 768
MESH = pl.DeviceIdType.MESH


def place():
    r = lax.axis_index("row")
    c = lax.axis_index("col")
    return r // 2, r % 2, c // 4, (c // 2) % 2, c % 2


def device(z, xh, y, xl, k):
    return (lax.rem(z + 4, 4) * 2 + xh, lax.rem(y + 4, 4) * 4 + xl * 2 + k)


def gather_kernel(w_ref, t_ref, g_ref, eye_ref, comb_ref, comb_t_ref, wb, tb, acc, ssem, rsem, lsem):
    z, xh, y, xl, k = place()
    half = {"w": wb.shape[1] // 2, "t": tb.shape[1] // 2}
    depth = w_ref.shape[1]
    k_cols = pl.ds(pl.multiple_of(k * depth, 128), depth)

    up_y, down_y = device(z, xh, y + 1, xl, k), device(z, xh, y - 1, xl, k)
    up_z, down_z = device(z + 1, xh, y, xl, k), device(z - 1, xh, y, xl, k)
    over_lo = device(z, xh, y, 1 - xl, k)
    over_hi = device(z, 1 - xh, y, xl, k)
    sib = device(z, xh, y, xl, 1 - k)

    barrier = pltpu.get_barrier_semaphore()
    peers = (up_y, down_y, up_z, down_z, over_lo, over_hi, sib)
    for peer in peers:
        pl.semaphore_signal(barrier, inc=1, device_id=peer, device_id_type=MESH)

    def slot(along, which):
        return lax.rem(along + 4, 4) * 2 + which

    def w_at(dy, e, h):
        e_xl = xl if e == 0 else 1 - xl
        return wb.at[slot(y + dy, e_xl), pl.ds(h * half["w"], half["w"]), k_cols]

    def t_at(dz, e, h):
        e_xh = xh if e == 0 else 1 - xh
        return tb.at[slot(z + dz, e_xh), pl.ds(h * half["t"], half["t"]), :]

    copies = {}

    def send(name, ref, peer, src=None):
        i = len(copies)
        copies[name] = pltpu.make_async_remote_copy(
            src_ref=ref if src is None else src,
            dst_ref=ref,
            send_sem=ssem.at[i],
            recv_sem=rsem.at[i],
            device_id=peer,
            device_id_type=MESH,
        )
        copies[name].start()

    def got(name):
        copies[name].wait_recv()

    own_w = pltpu.make_async_copy(w_ref, wb.at[slot(y, xl), :, k_cols], lsem.at[0])
    own_t = pltpu.make_async_copy(t_ref, tb.at[slot(z, xh)], lsem.at[1])
    own_w.start()
    own_t.start()
    pl.semaphore_wait(barrier, len(peers))

    def w_src(h):
        return w_ref.at[pl.ds(h * half["w"], half["w"]), :]

    def t_src(h):
        return t_ref.at[pl.ds(h * half["t"], half["t"]), :]

    for first in (0, 1):
        a, b = first, 1 - first
        send(f"y+0{a}", w_at(0, 0, a), up_y, w_src(a))
        send(f"y-0{b}", w_at(0, 0, b), down_y, w_src(b))
        send(f"z+0{a}", t_at(0, 0, a), up_z, t_src(a))
        send(f"z-0{b}", t_at(0, 0, b), down_z, t_src(b))
        send(f"xl{a}", w_at(0, 0, a), over_lo, w_src(a))
        send(f"xh{a}", t_at(0, 0, a), over_hi, t_src(a))
        send(f"s0{a}", w_at(0, 0, a), sib, w_src(a))

    acc[...] = jnp.zeros_like(acc)

    def class_of(distance, other):
        near = lax.rem(distance + 8, 4)
        ring = jnp.where(near == 0, 1, jnp.where(near == 2, 3, 2))
        return jnp.where(other == 0, 1, ring)

    def multiply(stage):
        def block(q, carry):
            far = jnp.maximum(
                class_of(q // 2 - y, lax.rem(q % 2 + xl, 2)),
                class_of(q // 2 - z, lax.rem(q % 2 + xh, 2)),
            )

            @pl.when(far == stage)
            def _():
                rows = 512

                def tile(s, inner):
                    at = pl.ds(pl.multiple_of(s * rows, rows), rows)
                    acc[at, :] += jnp.dot(
                        wb[q, at, :], tb[q], preferred_element_type=jnp.float32
                    )
                    return inner

                lax.fori_loop(0, wb.shape[1] // rows, tile, 0)

            return carry

        lax.fori_loop(0, 8, block, 0)

    got("y+00")
    send("fy+0", w_at(-1, 0, 0), up_y)
    got("z+00")
    send("fz+0", t_at(-1, 0, 0), up_z)
    got("y-01")
    send("fy-0", w_at(1, 0, 1), down_y)
    got("z-01")
    send("fz-0", t_at(1, 0, 1), down_z)
    send("s-0", w_at(-1, 0, 0), sib)
    send("s+1", w_at(1, 0, 1), sib)
    for h in (0, 1):
        got(f"xl{h}")
        send(f"y+1{h}", w_at(0, 1, h), up_y)
        send(f"y-1{h}", w_at(0, 1, h), down_y)
        got(f"xh{h}")
        send(f"z+1{h}", t_at(0, 1, h), up_z)
        send(f"z-1{h}", t_at(0, 1, h), down_z)
        send(f"sx{h}", w_at(0, 1, h), sib)
        if h == 0:
            got("y+01")
            send("s-1", w_at(-1, 0, 1), sib)
            got("y-00")
            send("s+0", w_at(1, 0, 0), sib)
            got("z+01")
            got("z-00")
    got("fy+0")
    send("s20", w_at(2, 0, 0), sib)
    got("fy-0")
    send("s21", w_at(2, 0, 1), sib)
    got("fz+0")
    got("fz-0")
    own_w.wait()
    own_t.wait()
    got("y+10")
    send("fy+1", w_at(-1, 1, 0), up_y)
    got("z+10")
    send("fz+1", t_at(-1, 1, 0), up_z)
    send("sx-0", w_at(-1, 1, 0), sib)
    for name in ("s00", "s01", "s-0", "s-1", "s+0", "s+1", "sx0", "sx1", "s20", "s21"):
        got(name)
    multiply(1)
    got("y-11")
    send("fy-1", w_at(1, 1, 1), down_y)
    got("z-11")
    send("fz-1", t_at(1, 1, 1), down_z)
    send("sx+1", w_at(1, 1, 1), sib)
    got("y+11")
    send("sx-1", w_at(-1, 1, 1), sib)
    got("y-10")
    send("sx+0", w_at(1, 1, 0), sib)
    got("z+11")
    got("z-10")
    for name in ("sx-0", "sx-1", "sx+0", "sx+1"):
        got(name)
    multiply(2)
    got("fy+1")
    send("sx20", w_at(2, 1, 0), sib)
    got("fy-1")
    send("sx21", w_at(2, 1, 1), sib)
    got("fz+1")
    got("fz-1")
    got("sx20")
    got("sx21")
    multiply(3)

    select = g_ref[...]
    eye = eye_ref[...]
    for j in range(acc.shape[1] // V):
        cols = pl.ds(j * V, V)

        def block(i, carry, cols=cols):
            rows = pl.ds(pl.multiple_of(i * V, V), V)
            cyc = acc[rows, cols]
            hi = cyc.astype(jnp.bfloat16)
            lo = (cyc - hi.astype(jnp.float32)).astype(jnp.bfloat16)

            def exchanged(part):
                moved = jnp.dot(select, part, preferred_element_type=jnp.float32).astype(jnp.bfloat16)
                return lax.dot_general(
                    select, moved, (((1,), (1,)), ((), ())), preferred_element_type=jnp.float32
                )

            comb = (2.0 * cyc - (exchanged(hi) + exchanged(lo))).astype(jnp.bfloat16)
            comb_ref[rows, cols] = comb
            comb_t_ref[cols, rows] = lax.dot_general(
                eye, comb, (((1,), (1,)), ((), ())), preferred_element_type=jnp.float32
            ).astype(jnp.bfloat16)
            return carry

        lax.fori_loop(0, acc.shape[0] // V, block, 0)
    for copy in copies.values():
        copy.wait_send()


def on_device(interaction, cycle_amps, tile_mask, virt_perm, occ_energy, virt_energy, old_amps):
    row_count, depth = interaction.shape
    out_cols = cycle_amps.shape[1]
    row = lax.axis_index("row")
    col = lax.axis_index("col")
    row_tiles = row_count // TILE
    flags = lax.dynamic_slice(tile_mask, (row * row_tiles, (col * depth) // TILE), (row_tiles, 1))
    masked = (
        interaction.reshape(row_tiles, TILE, depth) * flags[:, :, None].astype(jnp.bfloat16)
    ).reshape(row_count, depth)
    lanes = jnp.arange(V, dtype=jnp.int32)
    select = (virt_perm[:, None] == lanes[None, :]).astype(jnp.bfloat16)
    eye = (lanes[:, None] == lanes[None, :]).astype(jnp.bfloat16)
    combined, combined_t = pl.pallas_call(
        gather_kernel,
        name="gather_multiply",
        out_shape=(
            jax.ShapeDtypeStruct((row_count, out_cols), jnp.bfloat16),
            jax.ShapeDtypeStruct((out_cols, row_count), jnp.bfloat16),
        ),
        in_specs=[pl.BlockSpec(memory_space=pl.ANY)] * 2 + [pl.BlockSpec(memory_space=pltpu.VMEM)] * 2,
        out_specs=(pl.BlockSpec(memory_space=pltpu.VMEM),) * 2,
        scratch_shapes=[
            pltpu.VMEM((8, row_count, 2 * depth), jnp.bfloat16),
            pltpu.VMEM((8, cycle_amps.shape[0], out_cols), jnp.bfloat16),
            pltpu.VMEM((row_count, out_cols), jnp.float32),
            pltpu.SemaphoreType.DMA((48,)),
            pltpu.SemaphoreType.DMA((48,)),
            pltpu.SemaphoreType.DMA((2,)),
        ],
        compiler_params=pltpu.CompilerParams(
            collective_id=1, has_side_effects=True, vmem_limit_bytes=60 * 1024 * 1024
        ),
    )(masked, cycle_amps, select, eye)
    slab = lax.all_to_all(combined, "col", split_axis=0, concat_axis=1, tiled=True)
    columns = lax.all_to_all(slab, ("row", "col"), split_axis=1, concat_axis=0, tiled=True)
    paired = slab.astype(jnp.float32) + columns.T.astype(jnp.float32)
    slab_rows = slab.shape[0]
    total_cols = slab.shape[1]
    slab_index = row * lax.axis_size("col") + col
    global_rows = slab_index * slab_rows + jnp.arange(slab_rows, dtype=jnp.int32)
    row_energy = virt_energy[global_rows % V] - occ_energy[global_rows // V]
    pair_energy = (virt_energy[None, :] - occ_energy[:, None]).reshape(total_cols)
    denominator = row_energy[:, None] + pair_energy[None, :]
    return old_amps.astype(jnp.float32) + paired / denominator


def solution(mesh):
    placed = (P("row", "col"), P("row", "col"), P(), P(), P(), P(), P(("row", "col"), None))
    return jax.shard_map(
        on_device, mesh=mesh, in_specs=placed, out_specs=P(("row", "col"), None), check_vma=False
    )
```

```python
import functools

import jax
import jax.numpy as jnp
from jax import lax
from jax.experimental import pallas as pl
from jax.experimental.pallas import tpu as pltpu
from jax.sharding import PartitionSpec as P

V = 384
TILE = 768
MESH = pl.DeviceIdType.MESH


def place():
    r = lax.axis_index("row")
    c = lax.axis_index("col")
    return r // 2, r % 2, c // 4, (c // 2) % 2, c % 2


def device(z, xh, y, xl, k):
    return (lax.rem(z + 4, 4) * 2 + xh, lax.rem(y + 4, 4) * 4 + xl * 2 + k)


def cycle_kernel(
    mask_ref, perm_ref, w_ref, t_ref,
    rows_ref, cols_ref,
    wb, tb, acc, comb, comb_t, pick, ssem, rsem, lsem, row_sems, col_sems, land_sems,
):
    row, col = lax.axis_index("row"), lax.axis_index("col")
    z, xh, y, xl, k = place()
    half = {"w": wb.shape[1] // 2, "t": tb.shape[1] // 2}
    depth = w_ref.shape[1]
    tiles = acc.shape[0] // TILE
    k_cols = pl.ds(pl.multiple_of(k * depth, 128), depth)

    up_y, down_y = device(z, xh, y + 1, xl, k), device(z, xh, y - 1, xl, k)
    up_z, down_z = device(z + 1, xh, y, xl, k), device(z - 1, xh, y, xl, k)
    over_lo = device(z, xh, y, 1 - xl, k)
    over_hi = device(z, 1 - xh, y, xl, k)
    sib = device(z, xh, y, xl, 1 - k)

    barrier = pltpu.get_barrier_semaphore()

    def greet(peer):
        pl.semaphore_signal(barrier, inc=1, device_id=peer, device_id_type=MESH)

    for peer in (up_z, down_z, over_hi):
        greet(peer)

    def greet_row(step, carry):
        greet((row, lax.rem(col + step, 16)))
        return carry

    lax.fori_loop(1, 16, greet_row, 0)
    col_source = 2 * row + col // 8

    def greet_source(step, carry):
        @pl.when(jnp.logical_or(step != row, col_source != col))
        def _():
            greet((step, col_source))

        return carry

    lax.fori_loop(0, 8, greet_source, 0)
    expected = 3 + 15 + 8 - jnp.where(col_source == col, 1, 0)

    def slot(along, which):
        return lax.rem(along + 4, 4) * 2 + which

    def w_at(dy, e, h):
        e_xl = xl if e == 0 else 1 - xl
        return wb.at[slot(y + dy, e_xl), pl.ds(h * half["w"], half["w"]), k_cols]

    def t_at(dz, e, h):
        e_xh = xh if e == 0 else 1 - xh
        return tb.at[slot(z + dz, e_xh), pl.ds(h * half["t"], half["t"]), :]

    copies = {}

    def send(name, ref, peer, src=None):
        i = len(copies)
        copies[name] = pltpu.make_async_remote_copy(
            src_ref=ref if src is None else src,
            dst_ref=ref,
            send_sem=ssem.at[i],
            recv_sem=rsem.at[i],
            device_id=peer,
            device_id_type=MESH,
        )
        copies[name].start()

    def got(name):
        copies[name].wait_recv()

    own_w = pltpu.make_async_copy(w_ref, wb.at[slot(y, xl), :, k_cols], lsem.at[0])
    own_t = pltpu.make_async_copy(t_ref, tb.at[slot(z, xh)], lsem.at[1])
    own_w.start()
    own_t.start()
    pl.semaphore_wait(barrier, expected)

    def w_src(h):
        return w_ref.at[pl.ds(h * half["w"], half["w"]), :]

    def t_src(h):
        return t_ref.at[pl.ds(h * half["t"], half["t"]), :]

    for first in (0, 1):
        a, b = first, 1 - first
        send(f"y+0{a}", w_at(0, 0, a), up_y, w_src(a))
        send(f"y-0{b}", w_at(0, 0, b), down_y, w_src(b))
        send(f"z+0{a}", t_at(0, 0, a), up_z, t_src(a))
        send(f"z-0{b}", t_at(0, 0, b), down_z, t_src(b))
        send(f"xl{a}", w_at(0, 0, a), over_lo, w_src(a))
        send(f"xh{a}", t_at(0, 0, a), over_hi, t_src(a))
        send(f"s0{a}", w_at(0, 0, a), sib, w_src(a))

    acc[...] = jnp.zeros_like(acc)
    orbital = lax.broadcasted_iota(jnp.int32, pick.shape, 0)
    pick[...] = jnp.where(orbital == perm_ref[...], 1.0, 0.0).T.astype(jnp.bfloat16)

    def class_of(distance, other):
        near = lax.rem(distance + 8, 4)
        ring = jnp.where(near == 0, 1, jnp.where(near == 2, 3, 2))
        return jnp.where(other == 0, 1, ring)

    def multiply(stage):
        def block(q, carry):
            far = jnp.maximum(
                class_of(q // 2 - y, lax.rem(q % 2 + xl, 2)),
                class_of(q // 2 - z, lax.rem(q % 2 + xh, 2)),
            )

            @pl.when(far == stage)
            def _():
                def tile(p, inner):
                    at = pl.ds(pl.multiple_of(p * TILE, TILE), TILE)
                    kept = mask_ref[row * tiles + p, q].astype(jnp.float32)
                    acc[at, :] += kept * jnp.dot(
                        wb[q, at, :], tb[q], preferred_element_type=jnp.float32
                    )
                    return inner

                lax.fori_loop(0, tiles, tile, 0)

            return carry

        lax.fori_loop(0, 8, block, 0)

    got("y+00")
    send("fy+0", w_at(-1, 0, 0), up_y)
    got("z+00")
    send("fz+0", t_at(-1, 0, 0), up_z)
    got("y-01")
    send("fy-0", w_at(1, 0, 1), down_y)
    got("z-01")
    send("fz-0", t_at(1, 0, 1), down_z)
    send("s-0", w_at(-1, 0, 0), sib)
    send("s+1", w_at(1, 0, 1), sib)
    for h in (0, 1):
        got(f"xl{h}")
        send(f"y+1{h}", w_at(0, 1, h), up_y)
        send(f"y-1{h}", w_at(0, 1, h), down_y)
        got(f"xh{h}")
        send(f"z+1{h}", t_at(0, 1, h), up_z)
        send(f"z-1{h}", t_at(0, 1, h), down_z)
        send(f"sx{h}", w_at(0, 1, h), sib)
        if h == 0:
            got("y+01")
            send("s-1", w_at(-1, 0, 1), sib)
            got("y-00")
            send("s+0", w_at(1, 0, 0), sib)
            got("z+01")
            got("z-00")
    got("fy+0")
    send("s20", w_at(2, 0, 0), sib)
    got("fy-0")
    send("s21", w_at(2, 0, 1), sib)
    got("fz+0")
    got("fz-0")
    own_w.wait()
    own_t.wait()
    got("y+10")
    send("fy+1", w_at(-1, 1, 0), up_y)
    got("z+10")
    send("fz+1", t_at(-1, 1, 0), up_z)
    send("sx-0", w_at(-1, 1, 0), sib)
    for name in ("s00", "s01", "s-0", "s-1", "s+0", "s+1", "sx0", "sx1", "s20", "s21"):
        got(name)
    multiply(1)
    got("y-11")
    send("fy-1", w_at(1, 1, 1), down_y)
    got("z-11")
    send("fz-1", t_at(1, 1, 1), down_z)
    send("sx+1", w_at(1, 1, 1), sib)
    got("y+11")
    send("sx-1", w_at(-1, 1, 1), sib)
    got("y-10")
    send("sx+0", w_at(1, 1, 0), sib)
    got("z+11")
    got("z-10")
    for name in ("sx-0", "sx-1", "sx+0", "sx+1"):
        got(name)
    multiply(2)
    got("fy+1")
    send("sx20", w_at(2, 1, 0), sib)
    got("fy-1")
    send("sx21", w_at(2, 1, 1), sib)
    got("fz+1")
    got("fz-1")
    got("sx20")
    got("sx21")
    multiply(3)

    part = V // 4
    me = row * 16 + col
    row_base = row * acc.shape[0]
    col_base = col * acc.shape[1]

    def block_at(t):
        return lax.rem(y + t // 2, 4), lax.rem(t, 2)

    def exchange(t):
        i, j = block_at(t)
        rows = pl.ds(pl.multiple_of(i * V, V), V)
        cols = pl.ds(pl.multiple_of(j * V, V), V)
        select = pick[...]
        cyc = acc[rows, cols]
        hi = cyc.astype(jnp.bfloat16)
        lo = (cyc - hi.astype(jnp.float32)).astype(jnp.bfloat16)

        def exchanged(piece):
            moved = jnp.dot(select, piece, preferred_element_type=jnp.float32).astype(jnp.bfloat16)
            return lax.dot_general(
                select, moved, (((1,), (1,)), ((), ())), preferred_element_type=jnp.float32
            )

        combined = (2.0 * cyc - (exchanged(hi) + exchanged(lo))).astype(jnp.bfloat16)
        comb[rows, cols] = combined
        comb_t[cols, rows] = combined.T

    def pieces(t, s):
        i, j = block_at(t)
        n = t * 4 + s
        row_src = comb.at[
            pl.ds(pl.multiple_of(i * V + s * part, part), part), pl.ds(pl.multiple_of(j * V, V), V)
        ]
        row_dst = rows_ref.at[:, pl.ds(pl.multiple_of(col_base + j * V, V), V)]
        col_src = comb_t.at[
            pl.ds(pl.multiple_of(j * V + s * part, part), part), pl.ds(pl.multiple_of(i * V, V), V)
        ]
        col_dst = cols_ref.at[:, pl.ds(pl.multiple_of(row_base + i * V, V), V)]
        return (
            (row_src, row_dst, row_sems.at[n], land_sems.at[0], row, i * 4 + s),
            (col_src, col_dst, col_sems.at[n], land_sems.at[1], col // 2, lax.rem(col, 2) * 8 + j * 4 + s),
        )

    def each_piece(t, remote_step, local_step):
        def piece(s, carry):
            for src, dst, sent, landed, to_row, to_col in pieces(t, s):
                here = to_row * 16 + to_col == me

                @pl.when(here)
                def _():
                    local_step(pltpu.make_async_copy(src, dst, landed))

                @pl.when(jnp.logical_not(here))
                def _():
                    remote_step(
                        pltpu.make_async_remote_copy(
                            src_ref=src, dst_ref=dst, send_sem=sent, recv_sem=landed,
                            device_id=(to_row, to_col), device_id_type=MESH,
                        )
                    )

            return carry

        lax.fori_loop(0, 4, piece, 0)

    def start(t):
        each_piece(t, lambda copy: copy.start(), lambda copy: copy.start())

    def step(t, carry):
        exchange(t)

        @pl.when(t > 0)
        def _():
            start(t - 1)

        return carry

    lax.fori_loop(0, 8, step, 0)
    start(7)
    for copy in copies.values():
        copy.wait_send()

    def sent(t, carry):
        each_piece(t, lambda copy: copy.wait_send(), lambda copy: None)
        return carry

    lax.fori_loop(0, 8, sent, 0)
    pltpu.make_async_copy(rows_ref, rows_ref, land_sems.at[0]).wait()
    pltpu.make_async_copy(cols_ref, cols_ref, land_sems.at[1]).wait()


def on_device(interaction, cycle_amps, tile_mask, virt_perm, occ_energy, virt_energy, old_amps):
    row_count, depth = interaction.shape
    out_cols = cycle_amps.shape[1]
    row = lax.axis_index("row")
    col = lax.axis_index("col")
    total_cols = old_amps.shape[1]
    slab_rows = old_amps.shape[0]
    slab, columns = pl.pallas_call(
        cycle_kernel,
        name="cycle",
        out_shape=(jax.ShapeDtypeStruct((slab_rows, total_cols), jnp.bfloat16),) * 2,
        in_specs=[
            pl.BlockSpec(memory_space=pltpu.SMEM),
            pl.BlockSpec(memory_space=pltpu.VMEM),
            pl.BlockSpec(memory_space=pl.ANY),
            pl.BlockSpec(memory_space=pl.ANY),
        ],
        out_specs=(pl.BlockSpec(memory_space=pl.ANY),) * 2,
        scratch_shapes=[
            pltpu.VMEM((8, row_count, 2 * depth), jnp.bfloat16),
            pltpu.VMEM((8, cycle_amps.shape[0], out_cols), jnp.bfloat16),
            pltpu.VMEM((row_count, out_cols), jnp.float32),
            pltpu.VMEM((row_count, out_cols), jnp.bfloat16),
            pltpu.VMEM((out_cols, row_count), jnp.bfloat16),
            pltpu.VMEM((V, V), jnp.bfloat16),
            pltpu.SemaphoreType.DMA((48,)),
            pltpu.SemaphoreType.DMA((48,)),
            pltpu.SemaphoreType.DMA((2,)),
            pltpu.SemaphoreType.DMA((32,)),
            pltpu.SemaphoreType.DMA((32,)),
            pltpu.SemaphoreType.DMA((2,)),
        ],
        compiler_params=pltpu.CompilerParams(
            collective_id=1, has_side_effects=True, vmem_limit_bytes=60 * 1024 * 1024
        ),
    )(tile_mask, virt_perm.reshape(1, V), interaction, cycle_amps)
    paired = slab.astype(jnp.float32) + columns.astype(jnp.float32)
    slab_index = row * lax.axis_size("col") + col
    per_orbital = V // slab_rows
    row_energy = lax.dynamic_slice(
        virt_energy, (slab_index % per_orbital * slab_rows,), (slab_rows,)
    ) - lax.dynamic_slice(occ_energy, (slab_index // per_orbital,), (1,))
    pair_energy = (virt_energy[None, :] - occ_energy[:, None]).reshape(total_cols)
    denominator = row_energy[:, None] + pair_energy[None, :]
    return old_amps.astype(jnp.float32) + paired / denominator


def solution(mesh):
    placed = (P("row", "col"), P("row", "col"), P(), P(), P(), P(), P(("row", "col"), None))
    return jax.shard_map(
        on_device, mesh=mesh, in_specs=placed, out_specs=P(("row", "col"), None), check_vma=False
    )
```

```python
import functools

import jax
import jax.numpy as jnp
from jax import lax
from jax.experimental import pallas as pl
from jax.experimental.pallas import tpu as pltpu
from jax.sharding import PartitionSpec as P

V = 384
TILE = 768
MESH = pl.DeviceIdType.MESH


def place():
    r = lax.axis_index("row")
    c = lax.axis_index("col")
    return r // 2, r % 2, c // 4, (c // 2) % 2, c % 2


def device(z, xh, y, xl, k):
    return (lax.rem(z + 4, 4) * 2 + xh, lax.rem(y + 4, 4) * 4 + xl * 2 + k)


def cycle_kernel(
    mask_ref, perm_ref, w_ref, t_ref,
    rows_ref, cols_ref,
    wb, tb, acc, comb, comb_t, pick, mask, perm, ssem, rsem, lsem, row_sems, col_sems, land_sems,
):
    row, col = lax.axis_index("row"), lax.axis_index("col")
    z, xh, y, xl, k = place()
    half = {"w": wb.shape[1] // 2, "t": tb.shape[1] // 2}
    depth = w_ref.shape[1]
    tiles = acc.shape[0] // TILE
    k_cols = pl.ds(pl.multiple_of(k * depth, 128), depth)

    up_y, down_y = device(z, xh, y + 1, xl, k), device(z, xh, y - 1, xl, k)
    up_z, down_z = device(z + 1, xh, y, xl, k), device(z - 1, xh, y, xl, k)
    over_lo = device(z, xh, y, 1 - xl, k)
    over_hi = device(z, 1 - xh, y, xl, k)
    sib = device(z, xh, y, xl, 1 - k)

    barrier = pltpu.get_barrier_semaphore()

    def greet(peer):
        pl.semaphore_signal(barrier, inc=1, device_id=peer, device_id_type=MESH)

    for peer in (up_z, down_z, over_hi):
        greet(peer)

    def greet_row(step, carry):
        greet((row, lax.rem(col + step, 16)))
        return carry

    lax.fori_loop(1, 16, greet_row, 0)
    col_source = 2 * row + col // 8

    def greet_source(step, carry):
        @pl.when(jnp.logical_or(step != row, col_source != col))
        def _():
            greet((step, col_source))

        return carry

    lax.fori_loop(0, 8, greet_source, 0)
    expected = 3 + 15 + 8 - jnp.where(col_source == col, 1, 0)

    def slot(along, which):
        return lax.rem(along + 4, 4) * 2 + which

    def w_at(dy, e, h):
        e_xl = xl if e == 0 else 1 - xl
        return wb.at[slot(y + dy, e_xl), pl.ds(h * half["w"], half["w"]), k_cols]

    def t_at(dz, e, h):
        e_xh = xh if e == 0 else 1 - xh
        return tb.at[slot(z + dz, e_xh), pl.ds(h * half["t"], half["t"]), :]

    copies = {}

    def send(name, ref, peer, src=None):
        i = len(copies)
        copies[name] = pltpu.make_async_remote_copy(
            src_ref=ref if src is None else src,
            dst_ref=ref,
            send_sem=ssem.at[i],
            recv_sem=rsem.at[i],
            device_id=peer,
            device_id_type=MESH,
        )
        copies[name].start()

    def got(name):
        copies[name].wait_recv()

    own_w = pltpu.make_async_copy(w_ref, wb.at[slot(y, xl), :, k_cols], lsem.at[0])
    own_t = pltpu.make_async_copy(t_ref, tb.at[slot(z, xh)], lsem.at[1])
    small = (
        pltpu.make_async_copy(mask_ref, mask, lsem.at[2]),
        pltpu.make_async_copy(perm_ref, perm, lsem.at[3]),
    )
    for copy in (*small, own_w, own_t):
        copy.start()
    pl.semaphore_wait(barrier, expected)

    def w_src(h):
        return w_ref.at[pl.ds(h * half["w"], half["w"]), :]

    def t_src(h):
        return t_ref.at[pl.ds(h * half["t"], half["t"]), :]

    for first in (0, 1):
        a, b = first, 1 - first
        send(f"y+0{a}", w_at(0, 0, a), up_y, w_src(a))
        send(f"y-0{b}", w_at(0, 0, b), down_y, w_src(b))
        send(f"z+0{a}", t_at(0, 0, a), up_z, t_src(a))
        send(f"z-0{b}", t_at(0, 0, b), down_z, t_src(b))
        send(f"xl{a}", w_at(0, 0, a), over_lo, w_src(a))
        send(f"xh{a}", t_at(0, 0, a), over_hi, t_src(a))
        send(f"s0{a}", w_at(0, 0, a), sib, w_src(a))

    acc[...] = jnp.zeros_like(acc)
    for copy in small:
        copy.wait()
    orbital = lax.broadcasted_iota(jnp.int32, pick.shape, 0)
    pick[...] = jnp.where(orbital == perm[...].reshape(1, V), 1.0, 0.0).T.astype(jnp.bfloat16)

    def class_of(distance, other):
        near = lax.rem(distance + 8, 4)
        ring = jnp.where(near == 0, 1, jnp.where(near == 2, 3, 2))
        return jnp.where(other == 0, 1, ring)

    def multiply(stage):
        def block(q, carry):
            far = jnp.maximum(
                class_of(q // 2 - y, lax.rem(q % 2 + xl, 2)),
                class_of(q // 2 - z, lax.rem(q % 2 + xh, 2)),
            )

            @pl.when(far == stage)
            def _():
                def tile(p, inner):
                    at = pl.ds(pl.multiple_of(p * TILE, TILE), TILE)
                    kept = mask[q, row * tiles + p].astype(jnp.float32)
                    acc[at, :] += kept * jnp.dot(
                        wb[q, at, :], tb[q], preferred_element_type=jnp.float32
                    )
                    return inner

                lax.fori_loop(0, tiles, tile, 0)

            return carry

        lax.fori_loop(0, 8, block, 0)

    got("y+00")
    send("fy+0", w_at(-1, 0, 0), up_y)
    got("z+00")
    send("fz+0", t_at(-1, 0, 0), up_z)
    got("y-01")
    send("fy-0", w_at(1, 0, 1), down_y)
    got("z-01")
    send("fz-0", t_at(1, 0, 1), down_z)
    send("s-0", w_at(-1, 0, 0), sib)
    send("s+1", w_at(1, 0, 1), sib)
    for h in (0, 1):
        got(f"xl{h}")
        send(f"y+1{h}", w_at(0, 1, h), up_y)
        send(f"y-1{h}", w_at(0, 1, h), down_y)
        got(f"xh{h}")
        send(f"z+1{h}", t_at(0, 1, h), up_z)
        send(f"z-1{h}", t_at(0, 1, h), down_z)
        send(f"sx{h}", w_at(0, 1, h), sib)
        if h == 0:
            got("y+01")
            send("s-1", w_at(-1, 0, 1), sib)
            got("y-00")
            send("s+0", w_at(1, 0, 0), sib)
            got("z+01")
            got("z-00")
    got("fy+0")
    send("s20", w_at(2, 0, 0), sib)
    got("fy-0")
    send("s21", w_at(2, 0, 1), sib)
    got("fz+0")
    got("fz-0")
    own_w.wait()
    own_t.wait()
    got("y+10")
    send("fy+1", w_at(-1, 1, 0), up_y)
    got("z+10")
    send("fz+1", t_at(-1, 1, 0), up_z)
    send("sx-0", w_at(-1, 1, 0), sib)
    for name in ("s00", "s01", "s-0", "s-1", "s+0", "s+1", "sx0", "sx1", "s20", "s21"):
        got(name)
    multiply(1)
    got("y-11")
    send("fy-1", w_at(1, 1, 1), down_y)
    got("z-11")
    send("fz-1", t_at(1, 1, 1), down_z)
    send("sx+1", w_at(1, 1, 1), sib)
    got("y+11")
    send("sx-1", w_at(-1, 1, 1), sib)
    got("y-10")
    send("sx+0", w_at(1, 1, 0), sib)
    got("z+11")
    got("z-10")
    for name in ("sx-0", "sx-1", "sx+0", "sx+1"):
        got(name)
    multiply(2)
    got("fy+1")
    send("sx20", w_at(2, 1, 0), sib)
    got("fy-1")
    send("sx21", w_at(2, 1, 1), sib)
    got("fz+1")
    got("fz-1")
    got("sx20")
    got("sx21")
    multiply(3)

    part = V // 4
    me = row * 16 + col
    row_base = row * acc.shape[0]
    col_base = col * acc.shape[1]

    def block_at(t):
        n = t // 2
        hop = jnp.where(n == 0, 1, jnp.where(n == 1, 3, jnp.where(n == 2, 2, 0)))
        return lax.rem(y + jnp.where(k == 0, hop, 4 - hop), 4), lax.rem(t + 1 + y, 2)

    def exchange(t):
        i, j = block_at(t)
        rows = pl.ds(pl.multiple_of(i * V, V), V)
        cols = pl.ds(pl.multiple_of(j * V, V), V)
        select = pick[...]
        cyc = acc[rows, cols]
        hi = cyc.astype(jnp.bfloat16)
        lo = (cyc - hi.astype(jnp.float32)).astype(jnp.bfloat16)

        def exchanged(piece):
            moved = jnp.dot(select, piece, preferred_element_type=jnp.float32).astype(jnp.bfloat16)
            return lax.dot_general(
                select, moved, (((1,), (1,)), ((), ())), preferred_element_type=jnp.float32
            )

        combined = (2.0 * cyc - (exchanged(hi) + exchanged(lo))).astype(jnp.bfloat16)
        comb[rows, cols] = combined
        comb_t[cols, rows] = combined.T

    def pieces(t, s):
        i, j = block_at(t)
        n = t * 4 + s
        row_src = comb.at[
            pl.ds(pl.multiple_of(i * V + s * part, part), part), pl.ds(pl.multiple_of(j * V, V), V)
        ]
        row_dst = rows_ref.at[:, pl.ds(pl.multiple_of(col_base + j * V, V), V)]
        col_src = comb_t.at[
            pl.ds(pl.multiple_of(j * V + s * part, part), part), pl.ds(pl.multiple_of(i * V, V), V)
        ]
        col_dst = cols_ref.at[:, pl.ds(pl.multiple_of(row_base + i * V, V), V)]
        return (
            (row_src, row_dst, row_sems.at[n], land_sems.at[0], row, i * 4 + s),
            (col_src, col_dst, col_sems.at[n], land_sems.at[1], col // 2, lax.rem(col, 2) * 8 + j * 4 + s),
        )

    def each_piece(t, remote_step, local_step):
        def piece(s, carry):
            for src, dst, sent, landed, to_row, to_col in pieces(t, s):
                here = to_row * 16 + to_col == me

                @pl.when(here)
                def _():
                    local_step(pltpu.make_async_copy(src, dst, landed))

                @pl.when(jnp.logical_not(here))
                def _():
                    remote_step(
                        pltpu.make_async_remote_copy(
                            src_ref=src, dst_ref=dst, send_sem=sent, recv_sem=landed,
                            device_id=(to_row, to_col), device_id_type=MESH,
                        )
                    )

            return carry

        lax.fori_loop(0, 4, piece, 0)

    def start(t):
        each_piece(t, lambda copy: copy.start(), lambda copy: copy.start())

    def step(t, carry):
        exchange(t)

        @pl.when(t > 0)
        def _():
            start(t - 1)

        return carry

    lax.fori_loop(0, 8, step, 0)
    start(7)
    for copy in copies.values():
        copy.wait_send()

    def sent(t, carry):
        each_piece(t, lambda copy: copy.wait_send(), lambda copy: None)
        return carry

    lax.fori_loop(0, 8, sent, 0)
    pltpu.make_async_copy(rows_ref, rows_ref, land_sems.at[0]).wait()
    pltpu.make_async_copy(cols_ref, cols_ref, land_sems.at[1]).wait()


def update_kernel(
    rows_ref, cols_ref, old_ref, virt_ref, occ_ref, out_ref, old, out, virt, occ, in_sems, out_sems
):
    slab_rows = old.shape[0]
    chunks = in_sems.shape[0] - 2
    width = old.shape[1] // chunks
    slab = lax.axis_index("row") * 16 + lax.axis_index("col")
    small = (
        pltpu.make_async_copy(virt_ref, virt, in_sems.at[chunks]),
        pltpu.make_async_copy(occ_ref, occ, in_sems.at[chunks + 1]),
    )
    for copy in small:
        copy.start()

    def chunk_of(n):
        return (slice(None), pl.ds(n * width, width))

    reads = [
        pltpu.make_async_copy(old_ref.at[chunk_of(n)], old.at[chunk_of(n)], in_sems.at[n])
        for n in range(chunks)
    ]
    writes = [
        pltpu.make_async_copy(out.at[chunk_of(n)], out_ref.at[chunk_of(n)], out_sems.at[n])
        for n in range(chunks)
    ]
    for copy in reads:
        copy.start()
    for copy in small:
        copy.wait()
    per_orbital = V // slab_rows
    virtual = virt[...].reshape(1, V)
    lanes = lax.broadcasted_iota(jnp.int32, (slab_rows, V), 1)
    wanted = lax.broadcasted_iota(jnp.int32, (slab_rows, V), 0) + lax.rem(slab, per_orbital) * slab_rows
    row_energy = (
        jnp.sum(jnp.where(lanes == wanted, virtual, 0.0), axis=1, keepdims=True)
        - occ[slab // per_orbital]
    )
    for n in range(chunks):
        reads[n].wait()

        def orbital(j, carry):
            cols = pl.ds(pl.multiple_of(j * V, V), V)
            denominator = row_energy + (virtual - occ[j])
            paired = rows_ref[:, cols].astype(jnp.float32) + cols_ref[:, cols].astype(jnp.float32)
            out[:, cols] = old[:, cols].astype(jnp.float32) + paired / denominator
            return carry

        lax.fori_loop(n * (width // V), (n + 1) * (width // V), orbital, 0)
        writes[n].start()
    for copy in writes:
        copy.wait()


def on_device(interaction, cycle_amps, tile_mask, virt_perm, occ_energy, virt_energy, old_amps):
    row_count, depth = interaction.shape
    out_cols = cycle_amps.shape[1]
    slab_rows, total_cols = old_amps.shape
    rows, cols = pl.pallas_call(
        cycle_kernel,
        name="cycle",
        out_shape=(jax.ShapeDtypeStruct((slab_rows, total_cols), jnp.bfloat16),) * 2,
        in_specs=[pl.BlockSpec(memory_space=pltpu.HBM)] * 4,
        out_specs=(pl.BlockSpec(memory_space=pl.ANY),) * 2,
        scratch_shapes=[
            pltpu.VMEM((8, row_count, 2 * depth), jnp.bfloat16),
            pltpu.VMEM((8, cycle_amps.shape[0], out_cols), jnp.bfloat16),
            pltpu.VMEM((row_count, out_cols), jnp.float32),
            pltpu.VMEM((row_count, out_cols), jnp.bfloat16),
            pltpu.VMEM((out_cols, row_count), jnp.bfloat16),
            pltpu.VMEM((V, V), jnp.bfloat16),
            pltpu.SMEM(tile_mask.shape[::-1], jnp.int32),
            pltpu.VMEM((V,), jnp.int32),
            pltpu.SemaphoreType.DMA((48,)),
            pltpu.SemaphoreType.DMA((48,)),
            pltpu.SemaphoreType.DMA((4,)),
            pltpu.SemaphoreType.DMA((32,)),
            pltpu.SemaphoreType.DMA((32,)),
            pltpu.SemaphoreType.DMA((2,)),
        ],
        compiler_params=pltpu.CompilerParams(
            collective_id=1, has_side_effects=True, vmem_limit_bytes=44 * 1024 * 1024
        ),
    )(
        *(
            pltpu.with_memory_space_constraint(operand, pltpu.HBM)
            for operand in (tile_mask.T, virt_perm, interaction, cycle_amps)
        )
    )
    chunks = 4
    return pl.pallas_call(
        update_kernel,
        name="update",
        out_shape=jax.ShapeDtypeStruct((slab_rows, total_cols), jnp.float32),
        in_specs=[pl.BlockSpec(memory_space=pltpu.VMEM)] * 2 + [pl.BlockSpec(memory_space=pltpu.HBM)] * 3,
        out_specs=pl.BlockSpec(memory_space=pltpu.HBM),
        scratch_shapes=[
            pltpu.VMEM((slab_rows, total_cols), jnp.bfloat16),
            pltpu.VMEM((slab_rows, total_cols), jnp.float32),
            pltpu.VMEM((V,), jnp.float32),
            pltpu.SMEM((occ_energy.shape[0],), jnp.float32),
            pltpu.SemaphoreType.DMA((chunks + 2,)),
            pltpu.SemaphoreType.DMA((chunks,)),
        ],
        compiler_params=pltpu.CompilerParams(vmem_limit_bytes=12 * 1024 * 1024),
    )(rows, cols, old_amps, virt_energy, occ_energy)


def solution(mesh):
    placed = (P("row", "col"), P("row", "col"), P(), P(), P(), P(), P(("row", "col"), None))
    return jax.shard_map(
        on_device, mesh=mesh, in_specs=placed, out_specs=P(("row", "col"), None), check_vma=False
    )
```

```python
import functools

import jax
import jax.numpy as jnp
from jax import lax
from jax.experimental import pallas as pl
from jax.experimental.pallas import tpu as pltpu
from jax.sharding import PartitionSpec as P

V = 384
TILE = 768
MESH = pl.DeviceIdType.MESH


def place():
    r = lax.axis_index("row")
    c = lax.axis_index("col")
    return r // 2, r % 2, c // 4, (c // 2) % 2, c % 2


def device(z, xh, y, xl, k):
    return (lax.rem(z + 4, 4) * 2 + xh, lax.rem(y + 4, 4) * 4 + xl * 2 + k)


def cycle_kernel(
    mask_ref, perm_ref, w_ref, t_ref,
    rows_ref, cols_ref,
    wb, tb, acc, comb, comb_t, pick, mask, perm, ssem, rsem, lsem, row_sems, col_sems, land_sems,
):
    row, col = lax.axis_index("row"), lax.axis_index("col")
    z, xh, y, xl, k = place()
    depth = w_ref.shape[1]
    tiles = comb.shape[0] // TILE
    k_cols = pl.ds(pl.multiple_of(k * depth, 128), depth)

    up_y, down_y = device(z, xh, y + 1, xl, k), device(z, xh, y - 1, xl, k)
    up_z, down_z = device(z + 1, xh, y, xl, k), device(z - 1, xh, y, xl, k)
    over_lo = device(z, xh, y, 1 - xl, k)
    over_hi = device(z, 1 - xh, y, xl, k)
    sib = device(z, xh, y, xl, 1 - k)

    barrier = pltpu.get_barrier_semaphore()

    def greet(peer):
        pl.semaphore_signal(barrier, inc=1, device_id=peer, device_id_type=MESH)

    for peer in (up_z, down_z, over_hi):
        greet(peer)

    def greet_row(step, carry):
        greet((row, lax.rem(col + step, 16)))
        return carry

    lax.fori_loop(1, 16, greet_row, 0)
    col_source = 2 * row + col // 8

    def greet_source(step, carry):
        @pl.when(jnp.logical_or(step != row, col_source != col))
        def _():
            greet((step, col_source))

        return carry

    lax.fori_loop(0, 8, greet_source, 0)
    expected = 3 + 15 + 8 - jnp.where(col_source == col, 1, 0)

    def slot(along, which):
        return lax.rem(along + 4, 4) * 2 + which

    first = lax.rem(1 + y, 2)
    second = 1 - first

    def w_at(dy, e, rows):
        return wb.at[slot(y + dy, xl if e == 0 else 1 - xl), pl.ds(*rows), k_cols]

    def t_part(j, rows):
        return pl.ds(*rows), pl.ds(pl.multiple_of((second if j else first) * V, V), V)

    def t_at(dz, e, j, rows):
        return tb.at[(slot(z + dz, xh if e == 0 else 1 - xh), *t_part(j, rows))]

    copies = {}

    def send(name, ref, peer, src=None):
        i = len(copies)
        copies[name] = pltpu.make_async_remote_copy(
            src_ref=ref if src is None else src,
            dst_ref=ref,
            send_sem=ssem.at[i],
            recv_sem=rsem.at[i],
            device_id=peer,
            device_id_type=MESH,
        )
        copies[name].start()

    def got(*names):
        for name in names:
            copies[name].wait_recv()

    def w_own(name, peer, rows):
        send(name, w_at(0, 0, rows), peer, w_ref.at[pl.ds(*rows), :])

    def t_own(name, j, peer, rows):
        send(name, t_at(0, 0, j, rows), peer, t_ref.at[t_part(j, rows)])

    half = wb.shape[1] // 2
    w_a, w_b = (0, half), (half, half)
    w_up, w_mid, w_down = (0, V), (V, 2 * V), (3 * V, V)
    t_all, t_a, t_b = (0, 2 * V), (0, V), (V, V)

    small = (
        pltpu.make_async_copy(mask_ref, mask, lsem.at[2]),
        pltpu.make_async_copy(perm_ref, perm, lsem.at[3]),
    )
    own = (
        pltpu.make_async_copy(w_ref, wb.at[slot(y, xl), :, k_cols], lsem.at[0]),
        pltpu.make_async_copy(t_ref, tb.at[slot(z, xh)], lsem.at[1]),
    )
    for copy in small + own:
        copy.start()
    pl.semaphore_wait(barrier, expected)

    t_own("zua0", 0, up_z, t_a)
    t_own("zdb0", 0, down_z, t_b)
    w_own("yua", up_y, w_a)
    w_own("ydb", down_y, w_b)
    w_own("xa", over_lo, w_a)
    t_own("xh0", 0, over_hi, t_all)
    t_own("zub0", 0, up_z, t_b)
    t_own("zda0", 0, down_z, t_a)
    w_own("yub", up_y, w_b)
    w_own("yda", down_y, w_a)
    w_own("xb", over_lo, w_b)
    t_own("xh1", 1, over_hi, t_all)
    w_own("sa", sib, w_a)
    w_own("sb", sib, w_b)
    for copy in small + own:
        copy.wait()
    orbital = lax.broadcasted_iota(jnp.int32, pick.shape, 0)
    pick[...] = jnp.where(orbital == perm[...].reshape(1, V), 1.0, 0.0).T.astype(jnp.bfloat16)

    acc[...] = jnp.zeros_like(acc)

    def t_forward(j):
        got(f"zua{j}")
        send(f"zfu{j}", t_at(-1, 0, j, t_a), up_z)
        got(f"zdb{j}")
        send(f"zfd{j}", t_at(1, 0, j, t_b), down_z)

    def t_partner(j):
        got(f"xh{j}")
        send(f"zpu{j}", t_at(0, 1, j, t_all), up_z)
        send(f"zpd{j}", t_at(0, 1, j, t_all), down_z)

    def t_forward_partner(j):
        got(f"zpu{j}")
        send(f"zgu{j}", t_at(-1, 1, j, t_a), up_z)
        got(f"zpd{j}")
        send(f"zgd{j}", t_at(1, 1, j, t_b), down_z)

    def multiply(d, e, j):
        q = slot(y + d, xl if e == 0 else 1 - xl)
        cols = t_part(j, t_all)[1]

        def tile(p, inner):
            at = pl.ds(pl.multiple_of(p * TILE, TILE), TILE)
            kept = mask[q, row * tiles + p].astype(jnp.float32)
            acc[at, :] += kept * jnp.dot(
                wb[q, at, :], tb[q, :, cols], preferred_element_type=jnp.float32
            )
            return inner

        lax.fori_loop(0, tiles, tile, 0)

    def multiply_ring(steps, e, j):
        def one(n, carry):
            multiply(steps[0] + n * steps[2], e, j)
            return carry

        lax.fori_loop(0, steps[1], one, 0)

    part = V // 4
    me = row * 16 + col
    row_base = row * comb.shape[0]
    col_base = col * comb.shape[1]

    def exchange(i, j):
        rows = pl.ds(pl.multiple_of(i * V, V), V)
        cols = pl.ds(pl.multiple_of(j * V, V), V)
        select = pick[...]
        cyc = acc[rows, :]
        hi = cyc.astype(jnp.bfloat16)
        lo = (cyc - hi.astype(jnp.float32)).astype(jnp.bfloat16)

        def exchanged(piece):
            moved = jnp.dot(select, piece, preferred_element_type=jnp.float32).astype(jnp.bfloat16)
            return lax.dot_general(
                select, moved, (((1,), (1,)), ((), ())), preferred_element_type=jnp.float32
            )

        combined = (2.0 * cyc - (exchanged(hi) + exchanged(lo))).astype(jnp.bfloat16)
        comb[rows, cols] = combined
        comb_t[cols, rows] = combined.T

    def pieces(i, j, s):
        n = (i * 2 + j) * 4 + s
        row_src = comb.at[
            pl.ds(pl.multiple_of(i * V + s * part, part), part), pl.ds(pl.multiple_of(j * V, V), V)
        ]
        row_dst = rows_ref.at[:, pl.ds(pl.multiple_of(col_base + j * V, V), V)]
        col_src = comb_t.at[
            pl.ds(pl.multiple_of(j * V + s * part, part), part), pl.ds(pl.multiple_of(i * V, V), V)
        ]
        col_dst = cols_ref.at[:, pl.ds(pl.multiple_of(row_base + i * V, V), V)]
        return (
            (row_src, row_dst, row_sems.at[n], land_sems.at[0], row, i * 4 + s),
            (col_src, col_dst, col_sems.at[n], land_sems.at[1], col // 2, lax.rem(col, 2) * 8 + j * 4 + s),
        )

    def each_piece(i, j, remote_step, local_step):
        def piece(s, carry):
            for src, dst, sent, landed, to_row, to_col in pieces(i, j, s):
                here = to_row * 16 + to_col == me
                if local_step is not None:

                    @pl.when(here)
                    def _():
                        local_step(pltpu.make_async_copy(src, dst, landed))

                @pl.when(jnp.logical_not(here))
                def _():
                    remote_step(
                        pltpu.make_async_remote_copy(
                            src_ref=src, dst_ref=dst, send_sem=sent, recv_sem=landed,
                            device_id=(to_row, to_col), device_id_type=MESH,
                        )
                    )

            return carry

        lax.fori_loop(0, 4, piece, 0)

    def start(i, j):
        each_piece(i, j, lambda copy: copy.start(), lambda copy: copy.start())

    def turned(u):
        hop = jnp.where(u == 0, 1, jnp.where(u == 1, 3, jnp.where(u == 2, 2, 0)))
        return lax.rem(y + jnp.where(k == 0, hop, 4 - hop), 4)

    def leave(j):
        def step(u, carry):
            exchange(turned(u), j)

            @pl.when(u > 0)
            def _():
                start(turned(u - 1), j)

            return carry

        lax.fori_loop(0, 4, step, 0)
        start(turned(3), j)

    t_forward(0)
    got("yua")
    send("fu", w_at(-1, 0, w_a), up_y)
    send("sda", w_at(-1, 0, w_a), sib)
    got("ydb")
    send("fd", w_at(1, 0, w_b), down_y)
    send("sub", w_at(1, 0, w_b), sib)
    got("xa")
    send("pua", w_at(0, 1, w_a), up_y)
    send("pda", w_at(0, 1, w_a), down_y)
    send("sxa", w_at(0, 1, w_a), sib)
    t_partner(0)
    t_own("zua1", 1, up_z, t_a)
    t_own("zdb1", 1, down_z, t_b)
    got("yub")
    send("sdb", w_at(-1, 0, w_b), sib)
    got("yda")
    send("sua", w_at(1, 0, w_a), sib)
    got("xb")
    send("pub", w_at(0, 1, w_b), up_y)
    send("pdb", w_at(0, 1, w_b), down_y)
    send("sxb", w_at(0, 1, w_b), sib)
    got("fu", "fd")
    send("xf", w_at(2, 0, w_mid), over_lo)
    send("sf", w_at(2, 0, (0, 2 * half)), sib)
    t_forward_partner(0)
    t_own("zub1", 1, up_z, t_b)
    t_own("zda1", 1, down_z, t_a)
    t_partner(1)
    got("zub0", "zda0", "zfu0", "zfd0", "zgu0", "zgd0")
    got("sa", "sb", "sda", "sdb", "sua", "sub", "sxa", "sxb", "sf")
    multiply_ring((0, 2, 1), 0, 0)
    got("pua")
    send("gu", w_at(-1, 1, w_up), up_y)
    send("sxda", w_at(-1, 1, w_a), sib)
    t_forward(1)
    multiply_ring((2, 2, 1), 0, 0)
    got("pda")
    send("sxua", w_at(1, 1, w_a), sib)
    got("pdb")
    send("gd", w_at(1, 1, w_down), down_y)
    send("sxub", w_at(1, 1, w_b), sib)
    got("pub")
    send("sxdb", w_at(-1, 1, w_b), sib)
    got("xf")
    send("sxfm", w_at(2, 1, w_mid), sib)
    multiply_ring((0, 1, 1), 1, 0)
    t_forward_partner(1)
    got("gu")
    send("sxfu", w_at(2, 1, w_up), sib)
    got("gd")
    send("sxfd", w_at(2, 1, w_down), sib)
    got("sxda", "sxdb", "sxua", "sxub")
    multiply_ring((-1, 2, 2), 1, 0)
    got("sxfm", "sxfu", "sxfd")
    multiply_ring((2, 1, 1), 1, 0)
    leave(first)
    got("zub1", "zda1", "zfu1", "zfd1", "zgu1", "zgd1")
    acc[...] = jnp.zeros_like(acc)
    multiply_ring((0, 4, 1), 0, 1)
    multiply_ring((0, 4, 1), 1, 1)
    leave(second)
    for copy in copies.values():
        copy.wait_send()

    def sent(t, carry):
        each_piece(t // 2, lax.rem(t, 2), lambda copy: copy.wait_send(), None)
        return carry

    lax.fori_loop(0, 8, sent, 0)
    pltpu.make_async_copy(rows_ref, rows_ref, land_sems.at[0]).wait()
    pltpu.make_async_copy(cols_ref, cols_ref, land_sems.at[1]).wait()


def update_kernel(
    rows_ref, cols_ref, old_ref, virt_ref, occ_ref, out_ref, old, out, virt, occ, in_sems, out_sems
):
    slab_rows = old.shape[0]
    chunks = in_sems.shape[0] - 2
    width = old.shape[1] // chunks
    slab = lax.axis_index("row") * 16 + lax.axis_index("col")
    small = (
        pltpu.make_async_copy(virt_ref, virt, in_sems.at[chunks]),
        pltpu.make_async_copy(occ_ref, occ, in_sems.at[chunks + 1]),
    )
    for copy in small:
        copy.start()

    def chunk_of(n):
        return (slice(None), pl.ds(n * width, width))

    reads = [
        pltpu.make_async_copy(old_ref.at[chunk_of(n)], old.at[chunk_of(n)], in_sems.at[n])
        for n in range(chunks)
    ]
    writes = [
        pltpu.make_async_copy(out.at[chunk_of(n)], out_ref.at[chunk_of(n)], out_sems.at[n])
        for n in range(chunks)
    ]
    for copy in reads:
        copy.start()
    for copy in small:
        copy.wait()
    per_orbital = V // slab_rows
    virtual = virt[...].reshape(1, V)
    lanes = lax.broadcasted_iota(jnp.int32, (slab_rows, V), 1)
    wanted = lax.broadcasted_iota(jnp.int32, (slab_rows, V), 0) + lax.rem(slab, per_orbital) * slab_rows
    row_energy = (
        jnp.sum(jnp.where(lanes == wanted, virtual, 0.0), axis=1, keepdims=True)
        - occ[slab // per_orbital]
    )
    for n in range(chunks):
        reads[n].wait()

        def orbital(j, carry):
            cols = pl.ds(pl.multiple_of(j * V, V), V)
            denominator = row_energy + (virtual - occ[j])
            paired = rows_ref[:, cols].astype(jnp.float32) + cols_ref[:, cols].astype(jnp.float32)
            out[:, cols] = old[:, cols].astype(jnp.float32) + paired / denominator
            return carry

        lax.fori_loop(n * (width // V), (n + 1) * (width // V), orbital, 0)
        writes[n].start()
    for copy in writes:
        copy.wait()


def on_device(interaction, cycle_amps, tile_mask, virt_perm, occ_energy, virt_energy, old_amps):
    row_count, depth = interaction.shape
    out_cols = cycle_amps.shape[1]
    slab_rows, total_cols = old_amps.shape
    rows, cols = pl.pallas_call(
        cycle_kernel,
        name="cycle",
        out_shape=(jax.ShapeDtypeStruct((slab_rows, total_cols), jnp.bfloat16),) * 2,
        in_specs=[pl.BlockSpec(memory_space=pltpu.HBM)] * 4,
        out_specs=(pl.BlockSpec(memory_space=pl.ANY),) * 2,
        scratch_shapes=[
            pltpu.VMEM((8, row_count, 2 * depth), jnp.bfloat16),
            pltpu.VMEM((8, cycle_amps.shape[0], out_cols), jnp.bfloat16),
            pltpu.VMEM((row_count, V), jnp.float32),
            pltpu.VMEM((row_count, out_cols), jnp.bfloat16),
            pltpu.VMEM((out_cols, row_count), jnp.bfloat16),
            pltpu.VMEM((V, V), jnp.bfloat16),
            pltpu.SMEM(tile_mask.shape[::-1], jnp.int32),
            pltpu.VMEM((V,), jnp.int32),
            pltpu.SemaphoreType.DMA((64,)),
            pltpu.SemaphoreType.DMA((64,)),
            pltpu.SemaphoreType.DMA((4,)),
            pltpu.SemaphoreType.DMA((32,)),
            pltpu.SemaphoreType.DMA((32,)),
            pltpu.SemaphoreType.DMA((2,)),
        ],
        compiler_params=pltpu.CompilerParams(
            collective_id=1, has_side_effects=True, vmem_limit_bytes=44 * 1024 * 1024
        ),
    )(
        *(
            pltpu.with_memory_space_constraint(operand, pltpu.HBM)
            for operand in (tile_mask.T, virt_perm, interaction, cycle_amps)
        )
    )
    chunks = 4
    return pl.pallas_call(
        update_kernel,
        name="update",
        out_shape=jax.ShapeDtypeStruct((slab_rows, total_cols), jnp.float32),
        in_specs=[pl.BlockSpec(memory_space=pltpu.VMEM)] * 2 + [pl.BlockSpec(memory_space=pltpu.HBM)] * 3,
        out_specs=pl.BlockSpec(memory_space=pltpu.HBM),
        scratch_shapes=[
            pltpu.VMEM((slab_rows, total_cols), jnp.bfloat16),
            pltpu.VMEM((slab_rows, total_cols), jnp.float32),
            pltpu.VMEM((V,), jnp.float32),
            pltpu.SMEM((occ_energy.shape[0],), jnp.float32),
            pltpu.SemaphoreType.DMA((chunks + 2,)),
            pltpu.SemaphoreType.DMA((chunks,)),
        ],
        compiler_params=pltpu.CompilerParams(vmem_limit_bytes=12 * 1024 * 1024),
    )(rows, cols, old_amps, virt_energy, occ_energy)


def solution(mesh):
    placed = (P("row", "col"), P("row", "col"), P(), P(), P(), P(), P(("row", "col"), None))
    return jax.shard_map(
        on_device, mesh=mesh, in_specs=placed, out_specs=P(("row", "col"), None), check_vma=False
    )
```

```python
import functools

import jax
import jax.numpy as jnp
from jax import lax
from jax.experimental import pallas as pl
from jax.experimental.pallas import tpu as pltpu
from jax.sharding import PartitionSpec as P

V = 384
TILE = 768
MESH = pl.DeviceIdType.MESH


def place():
    r = lax.axis_index("row")
    c = lax.axis_index("col")
    return r // 2, r % 2, c // 4, (c // 2) % 2, c % 2


def device(z, xh, y, xl, k):
    return (lax.rem(z + 4, 4) * 2 + xh, lax.rem(y + 4, 4) * 4 + xl * 2 + k)


def cycle_kernel(
    mask_ref, perm_ref, w_ref, t_ref,
    rows_ref, cols_ref,
    wb, tb, acc, comb, comb_t, pick, mask, perm, ssem, rsem, lsem, row_sems, col_sems, land_sems,
):
    row, col = lax.axis_index("row"), lax.axis_index("col")
    z, xh, y, xl, k = place()
    depth = w_ref.shape[1]
    tiles = acc.shape[0] // TILE
    k_cols = pl.ds(pl.multiple_of(k * depth, 128), depth)

    up_y, down_y = device(z, xh, y + 1, xl, k), device(z, xh, y - 1, xl, k)
    up_z, down_z = device(z + 1, xh, y, xl, k), device(z - 1, xh, y, xl, k)
    over_lo = device(z, xh, y, 1 - xl, k)
    over_hi = device(z, 1 - xh, y, xl, k)
    sib = device(z, xh, y, xl, 1 - k)

    barrier = pltpu.get_barrier_semaphore()

    def greet(peer):
        pl.semaphore_signal(barrier, inc=1, device_id=peer, device_id_type=MESH)

    for peer in (up_z, down_z, over_hi):
        greet(peer)

    def greet_row(step, carry):
        greet((row, lax.rem(col + step, 16)))
        return carry

    lax.fori_loop(1, 16, greet_row, 0)
    col_source = 2 * row + col // 8

    def greet_source(step, carry):
        @pl.when(jnp.logical_or(step != row, col_source != col))
        def _():
            greet((step, col_source))

        return carry

    lax.fori_loop(0, 8, greet_source, 0)
    expected = 3 + 15 + 8 - jnp.where(col_source == col, 1, 0)

    def slot(along, which):
        return lax.rem(along + 4, 4) * 2 + which

    half = wb.shape[1] // 2
    w_parts = ((0, half), (half, half))
    t_parts = ((0, V), (V, V))
    w_far = ((0, 5 * half // 8), (5 * half // 8, 3 * half // 4), (11 * half // 8, 5 * half // 8))
    t_far = ((0, 5 * V // 8), (5 * V // 8, 3 * V // 4), (11 * V // 8, 5 * V // 8))

    def w_at(dy, e, part):
        return wb.at[slot(y + dy, xl if e == 0 else 1 - xl), pl.ds(*part), k_cols]

    def t_at(dz, e, part):
        return tb.at[slot(z + dz, xh if e == 0 else 1 - xh), pl.ds(*part), :]

    copies = {}

    def send(name, ref, peer, src=None):
        i = len(copies)
        copies[name] = pltpu.make_async_remote_copy(
            src_ref=ref if src is None else src,
            dst_ref=ref,
            send_sem=ssem.at[i],
            recv_sem=rsem.at[i],
            device_id=peer,
            device_id_type=MESH,
        )
        copies[name].start()

    def got(*names):
        for name in names:
            copies[name].wait_recv()

    own_w = pltpu.make_async_copy(w_ref, wb.at[slot(y, xl), :, k_cols], lsem.at[0])
    own_t = pltpu.make_async_copy(t_ref, tb.at[slot(z, xh)], lsem.at[1])
    small = (
        pltpu.make_async_copy(mask_ref, mask, lsem.at[2]),
        pltpu.make_async_copy(perm_ref, perm, lsem.at[3]),
    )
    for copy in (*small, own_w, own_t):
        copy.start()
    pl.semaphore_wait(barrier, expected)

    for first in (0, 1):
        a, b = first, 1 - first
        w_a, w_b, t_a, t_b = w_parts[a], w_parts[b], t_parts[a], t_parts[b]
        send(f"y+0{a}", w_at(0, 0, w_a), up_y, w_ref.at[pl.ds(*w_a), :])
        send(f"y-0{b}", w_at(0, 0, w_b), down_y, w_ref.at[pl.ds(*w_b), :])
        send(f"z+0{a}", t_at(0, 0, t_a), up_z, t_ref.at[pl.ds(*t_a), :])
        send(f"z-0{b}", t_at(0, 0, t_b), down_z, t_ref.at[pl.ds(*t_b), :])
        send(f"xl{a}", w_at(0, 0, w_a), over_lo, w_ref.at[pl.ds(*w_a), :])
        send(f"xh{a}", t_at(0, 0, t_a), over_hi, t_ref.at[pl.ds(*t_a), :])
        send(f"s0{a}", w_at(0, 0, w_a), sib, w_ref.at[pl.ds(*w_a), :])

    acc[...] = jnp.zeros_like(acc)
    for copy in small:
        copy.wait()
    orbital = lax.broadcasted_iota(jnp.int32, pick.shape, 0)
    pick[...] = jnp.where(orbital == perm[...].reshape(1, V), 1.0, 0.0).T.astype(jnp.bfloat16)

    def class_of(distance, other):
        near = lax.rem(distance + 8, 4)
        ring = jnp.where(near == 0, 1, jnp.where(near == 2, 3, 2))
        return jnp.where(other == 0, 1, ring)

    def farness(q):
        return jnp.maximum(
            class_of(q // 2 - y, lax.rem(q % 2 + xl, 2)),
            class_of(q // 2 - z, lax.rem(q % 2 + xh, 2)),
        )

    def add_product(q, start, size):
        at = pl.ds(pl.multiple_of(start, size), size)
        kept = mask[q, row * tiles + start // TILE].astype(jnp.float32)
        acc[at, :] += kept * jnp.dot(wb[q, at, :], tb[q], preferred_element_type=jnp.float32)

    def multiply(stage, begin=0, end=8):
        def block(q, carry):
            @pl.when(farness(q) == stage)
            def _():
                def tile(p, inner):
                    add_product(q, p * TILE, TILE)
                    return inner

                lax.fori_loop(0, tiles, tile, 0)

            return carry

        lax.fori_loop(begin, end, block, 0)

    def multiply_last(i):
        def block(q, carry):
            @pl.when(farness(q) == 3)
            def _():
                add_product(q, i * V, V)

            return carry

        lax.fori_loop(0, 8, block, 0)

    got("y+00")
    send("fy+0", w_at(-1, 0, w_parts[0]), up_y)
    got("z+00")
    send("fz+0", t_at(-1, 0, t_parts[0]), up_z)
    got("y-01")
    send("fy-0", w_at(1, 0, w_parts[1]), down_y)
    got("z-01")
    send("fz-0", t_at(1, 0, t_parts[1]), down_z)
    send("s-0", w_at(-1, 0, w_parts[0]), sib)
    send("s+1", w_at(1, 0, w_parts[1]), sib)

    def w_partner(h):
        got(f"xl{h}")
        send(f"y+1{h}", w_at(0, 1, w_parts[h]), up_y)
        send(f"y-1{h}", w_at(0, 1, w_parts[h]), down_y)
        send(f"sx{h}", w_at(0, 1, w_parts[h]), sib)

    def t_partner(h):
        got(f"xh{h}")
        send(f"z+1{h}", t_at(0, 1, t_parts[h]), up_z)
        send(f"z-1{h}", t_at(0, 1, t_parts[h]), down_z)

    w_partner(0)
    t_partner(0)
    got("y+01")
    send("s-1", w_at(-1, 0, w_parts[1]), sib)
    got("y-00")
    send("s+0", w_at(1, 0, w_parts[0]), sib)
    got("z+01", "z-00")
    w_partner(1)
    got("fy+0", "fy-0")
    send("xlf", w_at(2, 0, w_far[1]), over_lo)
    send("s2", w_at(2, 0, (0, 2 * half)), sib)
    got("fz+0", "fz-0")
    send("xhf", t_at(2, 0, t_far[1]), over_hi)
    t_partner(1)
    got("y+10")
    send("fy+1", w_at(-1, 1, w_far[0]), up_y)
    got("z+10")
    send("fz+1", t_at(-1, 1, t_far[0]), up_z)
    send("sx-0", w_at(-1, 1, w_parts[0]), sib)
    own_w.wait()
    own_t.wait()
    got("s00", "s01", "s-0", "s-1", "s+0", "s+1", "sx0", "sx1", "s2")
    multiply(1)
    got("y-11")
    send("fy-1", w_at(1, 1, w_far[2]), down_y)
    got("z-11")
    send("fz-1", t_at(1, 1, t_far[2]), down_z)
    send("sx+1", w_at(1, 1, w_parts[1]), sib)
    got("y+11")
    send("sx-1", w_at(-1, 1, w_parts[1]), sib)
    got("y-10")
    send("sx+0", w_at(1, 1, w_parts[0]), sib)
    got("z+11", "z-10")
    got("sx-0", "sx-1", "sx+0", "sx+1")
    multiply(2, 0, 4)
    got("fy+1")
    send("sf0", w_at(2, 1, w_far[0]), sib)
    got("xlf")
    send("sf1", w_at(2, 1, w_far[1]), sib)
    got("fy-1")
    send("sf2", w_at(2, 1, w_far[2]), sib)
    multiply(2, 4, 8)
    got("fz+1", "fz-1", "xhf")
    got("sf0", "sf1", "sf2")

    part = V // 4
    me = row * 16 + col
    row_base = row * acc.shape[0]
    col_base = col * acc.shape[1]

    def block_at(t):
        n = t // 2
        hop = jnp.where(n == 0, 1, jnp.where(n == 1, 3, jnp.where(n == 2, 2, 0)))
        return lax.rem(y + jnp.where(k == 0, hop, 4 - hop), 4), lax.rem(t + 1 + y, 2)

    def exchange(t):
        i, j = block_at(t)

        @pl.when(lax.rem(t, 2) == 0)
        def _():
            multiply_last(i)

        rows = pl.ds(pl.multiple_of(i * V, V), V)
        cols = pl.ds(pl.multiple_of(j * V, V), V)
        select = pick[...]
        cyc = acc[rows, cols]
        hi = cyc.astype(jnp.bfloat16)
        lo = (cyc - hi.astype(jnp.float32)).astype(jnp.bfloat16)

        def exchanged(piece):
            moved = jnp.dot(select, piece, preferred_element_type=jnp.float32).astype(jnp.bfloat16)
            return lax.dot_general(
                select, moved, (((1,), (1,)), ((), ())), preferred_element_type=jnp.float32
            )

        combined = (2.0 * cyc - (exchanged(hi) + exchanged(lo))).astype(jnp.bfloat16)
        comb[rows, cols] = combined
        comb_t[cols, rows] = combined.T

    def pieces(t, s):
        i, j = block_at(t)
        n = t * 4 + s
        row_src = comb.at[
            pl.ds(pl.multiple_of(i * V + s * part, part), part), pl.ds(pl.multiple_of(j * V, V), V)
        ]
        row_dst = rows_ref.at[:, pl.ds(pl.multiple_of(col_base + j * V, V), V)]
        col_src = comb_t.at[
            pl.ds(pl.multiple_of(j * V + s * part, part), part), pl.ds(pl.multiple_of(i * V, V), V)
        ]
        col_dst = cols_ref.at[:, pl.ds(pl.multiple_of(row_base + i * V, V), V)]
        return (
            (row_src, row_dst, row_sems.at[n], land_sems.at[0], row, i * 4 + s),
            (col_src, col_dst, col_sems.at[n], land_sems.at[1], col // 2, lax.rem(col, 2) * 8 + j * 4 + s),
        )

    def each_piece(t, remote_step, local_step):
        def piece(s, carry):
            for src, dst, sent, landed, to_row, to_col in pieces(t, s):
                here = to_row * 16 + to_col == me

                @pl.when(here)
                def _():
                    local_step(pltpu.make_async_copy(src, dst, landed))

                @pl.when(jnp.logical_not(here))
                def _():
                    remote_step(
                        pltpu.make_async_remote_copy(
                            src_ref=src, dst_ref=dst, send_sem=sent, recv_sem=landed,
                            device_id=(to_row, to_col), device_id_type=MESH,
                        )
                    )

            return carry

        lax.fori_loop(0, 4, piece, 0)

    def start(t):
        each_piece(t, lambda copy: copy.start(), lambda copy: copy.start())

    def step(t, carry):
        exchange(t)

        @pl.when(t > 0)
        def _():
            start(t - 1)

        return carry

    lax.fori_loop(0, 8, step, 0)
    start(7)
    for copy in copies.values():
        copy.wait_send()

    def sent(t, carry):
        each_piece(t, lambda copy: copy.wait_send(), lambda copy: None)
        return carry

    lax.fori_loop(0, 8, sent, 0)
    pltpu.make_async_copy(rows_ref, rows_ref, land_sems.at[0]).wait()
    pltpu.make_async_copy(cols_ref, cols_ref, land_sems.at[1]).wait()


def update_kernel(
    rows_ref, cols_ref, old_ref, virt_ref, occ_ref, out_ref, old, out, virt, occ, in_sems, out_sems
):
    slab_rows = old.shape[0]
    chunks = in_sems.shape[0] - 2
    width = old.shape[1] // chunks
    slab = lax.axis_index("row") * 16 + lax.axis_index("col")
    small = (
        pltpu.make_async_copy(virt_ref, virt, in_sems.at[chunks]),
        pltpu.make_async_copy(occ_ref, occ, in_sems.at[chunks + 1]),
    )
    for copy in small:
        copy.start()

    def chunk_of(n):
        return (slice(None), pl.ds(n * width, width))

    reads = [
        pltpu.make_async_copy(old_ref.at[chunk_of(n)], old.at[chunk_of(n)], in_sems.at[n])
        for n in range(chunks)
    ]
    writes = [
        pltpu.make_async_copy(out.at[chunk_of(n)], out_ref.at[chunk_of(n)], out_sems.at[n])
        for n in range(chunks)
    ]
    for copy in reads:
        copy.start()
    for copy in small:
        copy.wait()
    per_orbital = V // slab_rows
    virtual = virt[...].reshape(1, V)
    lanes = lax.broadcasted_iota(jnp.int32, (slab_rows, V), 1)
    wanted = lax.broadcasted_iota(jnp.int32, (slab_rows, V), 0) + lax.rem(slab, per_orbital) * slab_rows
    row_energy = (
        jnp.sum(jnp.where(lanes == wanted, virtual, 0.0), axis=1, keepdims=True)
        - occ[slab // per_orbital]
    )
    for n in range(chunks):
        reads[n].wait()

        def orbital(j, carry):
            cols = pl.ds(pl.multiple_of(j * V, V), V)
            denominator = row_energy + (virtual - occ[j])
            paired = rows_ref[:, cols].astype(jnp.float32) + cols_ref[:, cols].astype(jnp.float32)
            out[:, cols] = old[:, cols].astype(jnp.float32) + paired / denominator
            return carry

        lax.fori_loop(n * (width // V), (n + 1) * (width // V), orbital, 0)
        writes[n].start()
    for copy in writes:
        copy.wait()


def on_device(interaction, cycle_amps, tile_mask, virt_perm, occ_energy, virt_energy, old_amps):
    row_count, depth = interaction.shape
    out_cols = cycle_amps.shape[1]
    slab_rows, total_cols = old_amps.shape
    rows, cols = pl.pallas_call(
        cycle_kernel,
        name="cycle",
        out_shape=(jax.ShapeDtypeStruct((slab_rows, total_cols), jnp.bfloat16),) * 2,
        in_specs=[pl.BlockSpec(memory_space=pltpu.HBM)] * 4,
        out_specs=(pl.BlockSpec(memory_space=pl.ANY),) * 2,
        scratch_shapes=[
            pltpu.VMEM((8, row_count, 2 * depth), jnp.bfloat16),
            pltpu.VMEM((8, cycle_amps.shape[0], out_cols), jnp.bfloat16),
            pltpu.VMEM((row_count, out_cols), jnp.float32),
            pltpu.VMEM((row_count, out_cols), jnp.bfloat16),
            pltpu.VMEM((out_cols, row_count), jnp.bfloat16),
            pltpu.VMEM((V, V), jnp.bfloat16),
            pltpu.SMEM(tile_mask.shape[::-1], jnp.int32),
            pltpu.VMEM((V,), jnp.int32),
            pltpu.SemaphoreType.DMA((48,)),
            pltpu.SemaphoreType.DMA((48,)),
            pltpu.SemaphoreType.DMA((4,)),
            pltpu.SemaphoreType.DMA((32,)),
            pltpu.SemaphoreType.DMA((32,)),
            pltpu.SemaphoreType.DMA((2,)),
        ],
        compiler_params=pltpu.CompilerParams(
            collective_id=1, has_side_effects=True, vmem_limit_bytes=44 * 1024 * 1024
        ),
    )(
        *(
            pltpu.with_memory_space_constraint(operand, pltpu.HBM)
            for operand in (tile_mask.T, virt_perm, interaction, cycle_amps)
        )
    )
    chunks = 4
    return pl.pallas_call(
        update_kernel,
        name="update",
        out_shape=jax.ShapeDtypeStruct((slab_rows, total_cols), jnp.float32),
        in_specs=[pl.BlockSpec(memory_space=pltpu.VMEM)] * 2 + [pl.BlockSpec(memory_space=pltpu.HBM)] * 3,
        out_specs=pl.BlockSpec(memory_space=pltpu.HBM),
        scratch_shapes=[
            pltpu.VMEM((slab_rows, total_cols), jnp.bfloat16),
            pltpu.VMEM((slab_rows, total_cols), jnp.float32),
            pltpu.VMEM((V,), jnp.float32),
            pltpu.SMEM((occ_energy.shape[0],), jnp.float32),
            pltpu.SemaphoreType.DMA((chunks + 2,)),
            pltpu.SemaphoreType.DMA((chunks,)),
        ],
        compiler_params=pltpu.CompilerParams(vmem_limit_bytes=12 * 1024 * 1024),
    )(rows, cols, old_amps, virt_energy, occ_energy)


def solution(mesh):
    placed = (P("row", "col"), P("row", "col"), P(), P(), P(), P(), P(("row", "col"), None))
    return jax.shard_map(
        on_device, mesh=mesh, in_specs=placed, out_specs=P(("row", "col"), None), check_vma=False
    )
```

```python
import functools

import jax
import jax.numpy as jnp
from jax import lax
from jax.experimental import pallas as pl
from jax.experimental.pallas import tpu as pltpu
from jax.sharding import PartitionSpec as P

V = 384
TILE = 768
MESH = pl.DeviceIdType.MESH


def place():
    r = lax.axis_index("row")
    c = lax.axis_index("col")
    return r // 2, r % 2, c // 4, (c // 2) % 2, c % 2


def device(z, xh, y, xl, k):
    return (lax.rem(z + 4, 4) * 2 + xh, lax.rem(y + 4, 4) * 4 + xl * 2 + k)


def cycle_kernel(
    mask_ref, perm_ref, w_ref, t_ref,
    rows_ref, cols_ref,
    wb, tb, acc, comb, comb_t, pick, mask, perm, ssem, rsem, lsem, row_sems, col_sems, land_sems, near_sems,
):
    row, col = lax.axis_index("row"), lax.axis_index("col")
    z, xh, y, xl, k = place()
    depth = w_ref.shape[1]
    tiles = acc.shape[0] // TILE
    k_cols = pl.ds(pl.multiple_of(k * depth, 128), depth)

    up_y, down_y = device(z, xh, y + 1, xl, k), device(z, xh, y - 1, xl, k)
    up_z, down_z = device(z + 1, xh, y, xl, k), device(z - 1, xh, y, xl, k)
    over_lo = device(z, xh, y, 1 - xl, k)
    over_hi = device(z, 1 - xh, y, xl, k)
    sib = device(z, xh, y, xl, 1 - k)

    barrier = pltpu.get_barrier_semaphore()

    peers = (up_y, down_y, up_z, down_z, over_lo, over_hi, sib)
    for peer in peers:
        pl.semaphore_signal(barrier, inc=1, device_id=peer, device_id_type=MESH)

    def slot(along, which):
        return lax.rem(along + 4, 4) * 2 + which

    half = wb.shape[1] // 2
    w_parts = ((0, half), (half, half))
    t_parts = ((0, V), (V, V))
    w_far = ((0, 5 * half // 8), (5 * half // 8, 3 * half // 4), (11 * half // 8, 5 * half // 8))
    t_far = ((0, 5 * V // 8), (5 * V // 8, 3 * V // 4), (11 * V // 8, 5 * V // 8))

    def w_at(dy, e, part):
        return wb.at[slot(y + dy, xl if e == 0 else 1 - xl), pl.ds(*part), k_cols]

    def t_at(dz, e, part):
        return tb.at[slot(z + dz, xh if e == 0 else 1 - xh), pl.ds(*part), :]

    copies = {}

    def send(name, ref, peer, src=None):
        i = len(copies)
        copies[name] = pltpu.make_async_remote_copy(
            src_ref=ref if src is None else src,
            dst_ref=ref,
            send_sem=ssem.at[i],
            recv_sem=rsem.at[i],
            device_id=peer,
            device_id_type=MESH,
        )
        copies[name].start()

    def got(*names):
        for name in names:
            copies[name].wait_recv()

    own_w = pltpu.make_async_copy(w_ref, wb.at[slot(y, xl), :, k_cols], lsem.at[0])
    own_t = pltpu.make_async_copy(t_ref, tb.at[slot(z, xh)], lsem.at[1])
    small = (
        pltpu.make_async_copy(mask_ref, mask, lsem.at[2]),
        pltpu.make_async_copy(perm_ref, perm, lsem.at[3]),
    )
    for copy in (*small, own_w, own_t):
        copy.start()
    pl.semaphore_wait(barrier, len(peers))

    for first in (0, 1):
        a, b = first, 1 - first
        w_a, w_b, t_a, t_b = w_parts[a], w_parts[b], t_parts[a], t_parts[b]
        send(f"y+0{a}", w_at(0, 0, w_a), up_y, w_ref.at[pl.ds(*w_a), :])
        send(f"y-0{b}", w_at(0, 0, w_b), down_y, w_ref.at[pl.ds(*w_b), :])
        send(f"z+0{a}", t_at(0, 0, t_a), up_z, t_ref.at[pl.ds(*t_a), :])
        send(f"z-0{b}", t_at(0, 0, t_b), down_z, t_ref.at[pl.ds(*t_b), :])
        send(f"xl{a}", w_at(0, 0, w_a), over_lo, w_ref.at[pl.ds(*w_a), :])
        send(f"xh{a}", t_at(0, 0, t_a), over_hi, t_ref.at[pl.ds(*t_a), :])
        send(f"s0{a}", w_at(0, 0, w_a), sib, w_ref.at[pl.ds(*w_a), :])

    acc[...] = jnp.zeros_like(acc)
    for copy in small:
        copy.wait()
    orbital = lax.broadcasted_iota(jnp.int32, pick.shape, 0)
    pick[...] = jnp.where(orbital == perm[...].reshape(1, V), 1.0, 0.0).T.astype(jnp.bfloat16)

    def class_of(distance, other):
        near = lax.rem(distance + 8, 4)
        ring = jnp.where(near == 0, 1, jnp.where(near == 2, 3, 2))
        return jnp.where(other == 0, 1, ring)

    def farness(q):
        return jnp.maximum(
            class_of(q // 2 - y, lax.rem(q % 2 + xl, 2)),
            class_of(q // 2 - z, lax.rem(q % 2 + xh, 2)),
        )

    def add_product(q, start, size):
        at = pl.ds(pl.multiple_of(start, size), size)
        kept = mask[q, row * tiles + start // TILE].astype(jnp.float32)
        acc[at, :] += kept * jnp.dot(wb[q, at, :], tb[q], preferred_element_type=jnp.float32)

    def multiply(stage, begin=0, end=8):
        def block(q, carry):
            @pl.when(farness(q) == stage)
            def _():
                def tile(p, inner):
                    add_product(q, p * TILE, TILE)
                    return inner

                lax.fori_loop(0, tiles, tile, 0)

            return carry

        lax.fori_loop(begin, end, block, 0)

    def multiply_last(i):
        def block(q, carry):
            far = farness(q)

            @pl.when(jnp.logical_or(far == 3, jnp.logical_and(far == 2, q >= 4)))
            def _():
                add_product(q, i * V, V)

            return carry

        lax.fori_loop(0, 8, block, 0)

    def spread(n, carry):
        for peer in peers:
            pl.semaphore_signal(near_sems.at[n], inc=1, device_id=peer, device_id_type=MESH)
        pl.semaphore_wait(near_sems.at[n], len(peers))
        return carry

    lax.fori_loop(0, 6, spread, 0)

    got("y+00")
    send("fy+0", w_at(-1, 0, w_parts[0]), up_y)
    got("z+00")
    send("fz+0", t_at(-1, 0, t_parts[0]), up_z)
    got("y-01")
    send("fy-0", w_at(1, 0, w_parts[1]), down_y)
    got("z-01")
    send("fz-0", t_at(1, 0, t_parts[1]), down_z)
    send("s-0", w_at(-1, 0, w_parts[0]), sib)
    send("s+1", w_at(1, 0, w_parts[1]), sib)

    def w_partner(h):
        got(f"xl{h}")
        send(f"y+1{h}", w_at(0, 1, w_parts[h]), up_y)
        send(f"y-1{h}", w_at(0, 1, w_parts[h]), down_y)
        send(f"sx{h}", w_at(0, 1, w_parts[h]), sib)

    def t_partner(h):
        got(f"xh{h}")
        send(f"z+1{h}", t_at(0, 1, t_parts[h]), up_z)
        send(f"z-1{h}", t_at(0, 1, t_parts[h]), down_z)

    w_partner(0)
    t_partner(0)
    got("y+01")
    send("s-1", w_at(-1, 0, w_parts[1]), sib)
    got("y-00")
    send("s+0", w_at(1, 0, w_parts[0]), sib)
    got("z+01", "z-00")
    w_partner(1)
    got("fy+0", "fy-0")
    send("xlf", w_at(2, 0, w_far[1]), over_lo)
    send("s2", w_at(2, 0, (0, 2 * half)), sib)
    got("fz+0", "fz-0")
    send("xhf", t_at(2, 0, t_far[1]), over_hi)
    t_partner(1)
    got("y+10")
    send("fy+1", w_at(-1, 1, w_far[0]), up_y)
    got("z+10")
    send("fz+1", t_at(-1, 1, t_far[0]), up_z)
    send("sx-0", w_at(-1, 1, w_parts[0]), sib)
    own_w.wait()
    own_t.wait()
    got("s00", "s01", "s-0", "s-1", "s+0", "s+1", "sx0", "sx1", "s2")
    multiply(1)
    got("y-11")
    send("fy-1", w_at(1, 1, w_far[2]), down_y)
    got("z-11")
    send("fz-1", t_at(1, 1, t_far[2]), down_z)
    send("sx+1", w_at(1, 1, w_parts[1]), sib)
    got("y+11")
    send("sx-1", w_at(-1, 1, w_parts[1]), sib)
    got("y-10")
    send("sx+0", w_at(1, 1, w_parts[0]), sib)
    got("z+11", "z-10")
    got("sx-0", "sx-1", "sx+0", "sx+1")
    multiply(2, 0, 4)
    got("fy+1")
    send("sf0", w_at(2, 1, w_far[0]), sib)
    got("xlf")
    send("sf1", w_at(2, 1, w_far[1]), sib)
    got("fy-1")
    send("sf2", w_at(2, 1, w_far[2]), sib)
    got("fz+1", "fz-1", "xhf")
    got("sf0", "sf1", "sf2")

    part = V // 4
    me = row * 16 + col
    row_base = row * acc.shape[0]
    col_base = col * acc.shape[1]

    def block_at(t):
        n = t // 2
        hop = jnp.where(n == 0, 1, jnp.where(n == 1, 3, jnp.where(n == 2, 2, 0)))
        return lax.rem(y + jnp.where(k == 0, hop, 4 - hop), 4), lax.rem(t + 1 + y, 2)

    def exchange(t):
        i, j = block_at(t)

        @pl.when(lax.rem(t, 2) == 0)
        def _():
            multiply_last(i)

        rows = pl.ds(pl.multiple_of(i * V, V), V)
        cols = pl.ds(pl.multiple_of(j * V, V), V)
        select = pick[...]
        cyc = acc[rows, cols]
        hi = cyc.astype(jnp.bfloat16)
        lo = (cyc - hi.astype(jnp.float32)).astype(jnp.bfloat16)

        def exchanged(piece):
            moved = jnp.dot(select, piece, preferred_element_type=jnp.float32).astype(jnp.bfloat16)
            return lax.dot_general(
                select, moved, (((1,), (1,)), ((), ())), preferred_element_type=jnp.float32
            )

        combined = (2.0 * cyc - (exchanged(hi) + exchanged(lo))).astype(jnp.bfloat16)
        comb[rows, cols] = combined
        comb_t[cols, rows] = combined.T

    def pieces(t, s):
        i, j = block_at(t)
        n = t * 4 + s
        row_src = comb.at[
            pl.ds(pl.multiple_of(i * V + s * part, part), part), pl.ds(pl.multiple_of(j * V, V), V)
        ]
        row_dst = rows_ref.at[:, pl.ds(pl.multiple_of(col_base + j * V, V), V)]
        col_src = comb_t.at[
            pl.ds(pl.multiple_of(j * V + s * part, part), part), pl.ds(pl.multiple_of(i * V, V), V)
        ]
        col_dst = cols_ref.at[:, pl.ds(pl.multiple_of(row_base + i * V, V), V)]
        return (
            (row_src, row_dst, row_sems.at[n], land_sems.at[0], row, i * 4 + s),
            (col_src, col_dst, col_sems.at[n], land_sems.at[1], col // 2, lax.rem(col, 2) * 8 + j * 4 + s),
        )

    def each_piece(t, remote_step, local_step):
        def piece(s, carry):
            for src, dst, sent, landed, to_row, to_col in pieces(t, s):
                here = to_row * 16 + to_col == me

                @pl.when(here)
                def _():
                    local_step(pltpu.make_async_copy(src, dst, landed))

                @pl.when(jnp.logical_not(here))
                def _():
                    remote_step(
                        pltpu.make_async_remote_copy(
                            src_ref=src, dst_ref=dst, send_sem=sent, recv_sem=landed,
                            device_id=(to_row, to_col), device_id_type=MESH,
                        )
                    )

            return carry

        lax.fori_loop(0, 4, piece, 0)

    def start(t):
        each_piece(t, lambda copy: copy.start(), lambda copy: copy.start())

    def step(t, carry):
        exchange(t)
        start(t)
        return carry

    lax.fori_loop(0, 8, step, 0)
    for copy in copies.values():
        copy.wait_send()

    def sent(t, carry):
        each_piece(t, lambda copy: copy.wait_send(), lambda copy: None)
        return carry

    lax.fori_loop(0, 8, sent, 0)
    pltpu.make_async_copy(rows_ref, rows_ref, land_sems.at[0]).wait()
    pltpu.make_async_copy(cols_ref, cols_ref, land_sems.at[1]).wait()


def update_kernel(
    rows_ref, cols_ref, old_ref, virt_ref, occ_ref, out_ref, old, out, virt, occ, in_sems, out_sems
):
    slab_rows = old.shape[0]
    chunks = in_sems.shape[0] - 2
    width = old.shape[1] // chunks
    slab = lax.axis_index("row") * 16 + lax.axis_index("col")
    small = (
        pltpu.make_async_copy(virt_ref, virt, in_sems.at[chunks]),
        pltpu.make_async_copy(occ_ref, occ, in_sems.at[chunks + 1]),
    )
    for copy in small:
        copy.start()

    def chunk_of(n):
        return (slice(None), pl.ds(n * width, width))

    reads = [
        pltpu.make_async_copy(old_ref.at[chunk_of(n)], old.at[chunk_of(n)], in_sems.at[n])
        for n in range(chunks)
    ]
    writes = [
        pltpu.make_async_copy(out.at[chunk_of(n)], out_ref.at[chunk_of(n)], out_sems.at[n])
        for n in range(chunks)
    ]
    for copy in reads:
        copy.start()
    for copy in small:
        copy.wait()
    per_orbital = V // slab_rows
    virtual = virt[...].reshape(1, V)
    lanes = lax.broadcasted_iota(jnp.int32, (slab_rows, V), 1)
    wanted = lax.broadcasted_iota(jnp.int32, (slab_rows, V), 0) + lax.rem(slab, per_orbital) * slab_rows
    row_energy = (
        jnp.sum(jnp.where(lanes == wanted, virtual, 0.0), axis=1, keepdims=True)
        - occ[slab // per_orbital]
    )
    for n in range(chunks):
        reads[n].wait()

        def orbital(j, carry):
            cols = pl.ds(pl.multiple_of(j * V, V), V)
            denominator = row_energy + (virtual - occ[j])
            paired = rows_ref[:, cols].astype(jnp.float32) + cols_ref[:, cols].astype(jnp.float32)
            out[:, cols] = old[:, cols].astype(jnp.float32) + paired / denominator
            return carry

        lax.fori_loop(n * (width // V), (n + 1) * (width // V), orbital, 0)
        writes[n].start()
    for copy in writes:
        copy.wait()


def on_device(interaction, cycle_amps, tile_mask, virt_perm, occ_energy, virt_energy, old_amps):
    row_count, depth = interaction.shape
    out_cols = cycle_amps.shape[1]
    slab_rows, total_cols = old_amps.shape
    rows, cols = pl.pallas_call(
        cycle_kernel,
        name="cycle",
        out_shape=(jax.ShapeDtypeStruct((slab_rows, total_cols), jnp.bfloat16),) * 2,
        in_specs=[pl.BlockSpec(memory_space=pltpu.HBM)] * 4,
        out_specs=(pl.BlockSpec(memory_space=pl.ANY),) * 2,
        scratch_shapes=[
            pltpu.VMEM((8, row_count, 2 * depth), jnp.bfloat16),
            pltpu.VMEM((8, cycle_amps.shape[0], out_cols), jnp.bfloat16),
            pltpu.VMEM((row_count, out_cols), jnp.float32),
            pltpu.VMEM((row_count, out_cols), jnp.bfloat16),
            pltpu.VMEM((out_cols, row_count), jnp.bfloat16),
            pltpu.VMEM((V, V), jnp.bfloat16),
            pltpu.SMEM(tile_mask.shape[::-1], jnp.int32),
            pltpu.VMEM((V,), jnp.int32),
            pltpu.SemaphoreType.DMA((48,)),
            pltpu.SemaphoreType.DMA((48,)),
            pltpu.SemaphoreType.DMA((4,)),
            pltpu.SemaphoreType.DMA((32,)),
            pltpu.SemaphoreType.DMA((32,)),
            pltpu.SemaphoreType.DMA((2,)),
            pltpu.SemaphoreType.REGULAR((6,)),
        ],
        compiler_params=pltpu.CompilerParams(
            collective_id=1, has_side_effects=True, vmem_limit_bytes=44 * 1024 * 1024
        ),
    )(
        *(
            pltpu.with_memory_space_constraint(operand, pltpu.HBM)
            for operand in (tile_mask.T, virt_perm, interaction, cycle_amps)
        )
    )
    chunks = 4
    return pl.pallas_call(
        update_kernel,
        name="update",
        out_shape=jax.ShapeDtypeStruct((slab_rows, total_cols), jnp.float32),
        in_specs=[pl.BlockSpec(memory_space=pltpu.VMEM)] * 2 + [pl.BlockSpec(memory_space=pltpu.HBM)] * 3,
        out_specs=pl.BlockSpec(memory_space=pltpu.HBM),
        scratch_shapes=[
            pltpu.VMEM((slab_rows, total_cols), jnp.bfloat16),
            pltpu.VMEM((slab_rows, total_cols), jnp.float32),
            pltpu.VMEM((V,), jnp.float32),
            pltpu.SMEM((occ_energy.shape[0],), jnp.float32),
            pltpu.SemaphoreType.DMA((chunks + 2,)),
            pltpu.SemaphoreType.DMA((chunks,)),
        ],
        compiler_params=pltpu.CompilerParams(vmem_limit_bytes=12 * 1024 * 1024),
    )(rows, cols, old_amps, virt_energy, occ_energy)


def solution(mesh):
    placed = (P("row", "col"), P("row", "col"), P(), P(), P(), P(), P(("row", "col"), None))
    return jax.shard_map(
        on_device, mesh=mesh, in_specs=placed, out_specs=P(("row", "col"), None), check_vma=False
    )
```

```python
import functools

import jax
import jax.numpy as jnp
from jax import lax
from jax.experimental import pallas as pl
from jax.experimental.pallas import tpu as pltpu
from jax.sharding import PartitionSpec as P

V = 384
TILE = 768
MESH = pl.DeviceIdType.MESH


def place():
    r = lax.axis_index("row")
    c = lax.axis_index("col")
    return r // 2, r % 2, c // 4, (c // 2) % 2, c % 2


def device(z, xh, y, xl, k):
    return (lax.rem(z + 4, 4) * 2 + xh, lax.rem(y + 4, 4) * 4 + xl * 2 + k)


def cycle_kernel(
    mask_ref, perm_ref, w_ref, t_ref,
    rows_ref, cols_ref,
    wb, tb, acc, comb, comb_t, pick, mask, perm, ssem, rsem, lsem, row_sems, col_sems, land_sems, near_sems,
):
    row, col = lax.axis_index("row"), lax.axis_index("col")
    z, xh, y, xl, k = place()
    depth = w_ref.shape[1]
    tiles = acc.shape[0] // TILE
    k_cols = pl.ds(pl.multiple_of(k * depth, 128), depth)

    up_y, down_y = device(z, xh, y + 1, xl, k), device(z, xh, y - 1, xl, k)
    up_z, down_z = device(z + 1, xh, y, xl, k), device(z - 1, xh, y, xl, k)
    over_lo = device(z, xh, y, 1 - xl, k)
    over_hi = device(z, 1 - xh, y, xl, k)
    sib = device(z, xh, y, xl, 1 - k)

    barrier = pltpu.get_barrier_semaphore()

    peers = (up_y, down_y, up_z, down_z, over_lo, over_hi, sib)
    for peer in peers:
        pl.semaphore_signal(barrier, inc=1, device_id=peer, device_id_type=MESH)

    def slot(along, which):
        return lax.rem(along + 4, 4) * 2 + which

    half = wb.shape[1] // 2
    w_parts = ((0, half), (half, half))
    t_parts = ((0, V), (V, V))
    w_far = ((0, 288), (576, 960), (288, 288))
    t_far = ((0, 288), (576, 192), (288, 288))
    w_cross = {"0": (0, half), "1": (half, half // 2), "2": (3 * half // 2, half // 2)}
    t_cross = {"0": (0, V), "1": (V, V // 2), "2": (3 * V // 2, V // 2)}

    def w_at(dy, e, part):
        return wb.at[slot(y + dy, xl if e == 0 else 1 - xl), pl.ds(*part), k_cols]

    def t_at(dz, e, part):
        return tb.at[slot(z + dz, xh if e == 0 else 1 - xh), pl.ds(*part), :]

    copies = {}

    def send(name, ref, peer, src=None):
        i = len(copies)
        copies[name] = pltpu.make_async_remote_copy(
            src_ref=ref if src is None else src,
            dst_ref=ref,
            send_sem=ssem.at[i],
            recv_sem=rsem.at[i],
            device_id=peer,
            device_id_type=MESH,
        )
        copies[name].start()

    def got(*names):
        for name in names:
            copies[name].wait_recv()

    own_w = pltpu.make_async_copy(w_ref, wb.at[slot(y, xl), :, k_cols], lsem.at[0])
    own_t = pltpu.make_async_copy(t_ref, tb.at[slot(z, xh)], lsem.at[1])
    small = (
        pltpu.make_async_copy(mask_ref, mask, lsem.at[2]),
        pltpu.make_async_copy(perm_ref, perm, lsem.at[3]),
    )
    for copy in (*small, own_w, own_t):
        copy.start()
    pl.semaphore_wait(barrier, len(peers))

    for first in (0, 1):
        a, b = first, 1 - first
        w_a, w_b, t_a, t_b = w_parts[a], w_parts[b], t_parts[a], t_parts[b]
        send(f"y+0{a}", w_at(0, 0, w_a), up_y, w_ref.at[pl.ds(*w_a), :])
        send(f"y-0{b}", w_at(0, 0, w_b), down_y, w_ref.at[pl.ds(*w_b), :])
        send(f"z+0{a}", t_at(0, 0, t_a), up_z, t_ref.at[pl.ds(*t_a), :])
        send(f"z-0{b}", t_at(0, 0, t_b), down_z, t_ref.at[pl.ds(*t_b), :])
        for h in ("0",) if first == 0 else ("1", "2"):
            w_h, t_h = w_cross[h], t_cross[h]
            send(f"xl{h}", w_at(0, 0, w_h), over_lo, w_ref.at[pl.ds(*w_h), :])
            send(f"xh{h}", t_at(0, 0, t_h), over_hi, t_ref.at[pl.ds(*t_h), :])
        send(f"s0{a}", w_at(0, 0, w_a), sib, w_ref.at[pl.ds(*w_a), :])

    acc[...] = jnp.zeros_like(acc)
    for copy in small:
        copy.wait()
    orbital = lax.broadcasted_iota(jnp.int32, pick.shape, 0)
    pick[...] = jnp.where(orbital == perm[...].reshape(1, V), 1.0, 0.0).T.astype(jnp.bfloat16)

    def class_of(distance, other):
        near = lax.rem(distance + 8, 4)
        ring = jnp.where(near == 0, 1, jnp.where(near == 2, 3, 2))
        return jnp.where(other == 0, 0, ring)

    def farness(q):
        return jnp.maximum(
            class_of(q // 2 - y, lax.rem(q % 2 + xl, 2)),
            class_of(q // 2 - z, lax.rem(q % 2 + xh, 2)),
        )

    def add_product(q, start, size):
        at = pl.ds(pl.multiple_of(start, size), size)
        kept = mask[q, row * tiles + start // TILE].astype(jnp.float32)
        acc[at, :] += kept * jnp.dot(wb[q, at, :], tb[q], preferred_element_type=jnp.float32)

    def multiply(stage, begin=0, end=8):
        def block(q, carry):
            @pl.when(farness(q) == stage)
            def _():
                def tile(p, inner):
                    add_product(q, p * TILE, TILE)
                    return inner

                lax.fori_loop(0, tiles, tile, 0)

            return carry

        lax.fori_loop(begin, end, block, 0)

    def block_at(t):
        n = t // 2
        hop = jnp.where(n == 0, 1, jnp.where(n == 1, 3, jnp.where(n == 2, 2, 0)))
        return lax.rem(y + jnp.where(k == 0, hop, 4 - hop), 4), lax.rem(t + 1 + y, 2)

    late = slot(z + 2, 1 - xh)

    def multiply_rest(i):
        def block(q, carry):
            far = farness(q)
            left = jnp.logical_or(far == 3, jnp.logical_and(far == 2, q >= 4))

            @pl.when(jnp.logical_and(left, q != late))
            def _():
                add_product(q, i * V, V)

            return carry

        lax.fori_loop(0, 8, block, 0)

    def spread(n, carry):
        for peer in peers:
            pl.semaphore_signal(near_sems.at[n], inc=1, device_id=peer, device_id_type=MESH)
        pl.semaphore_wait(near_sems.at[n], len(peers))
        return carry

    lax.fori_loop(0, 6, spread, 0)

    got("y+00")
    send("fy+0", w_at(-1, 0, w_parts[0]), up_y)
    got("z+00")
    send("fz+0", t_at(-1, 0, t_parts[0]), up_z)
    got("y-01")
    send("fy-0", w_at(1, 0, w_parts[1]), down_y)
    got("z-01")
    send("fz-0", t_at(1, 0, t_parts[1]), down_z)
    send("s-0", w_at(-1, 0, w_parts[0]), sib)
    send("s+1", w_at(1, 0, w_parts[1]), sib)

    def w_partner(h):
        got(f"xl{h}")
        send(f"y+1{h}", w_at(0, 1, w_cross[h]), up_y)
        send(f"y-1{h}", w_at(0, 1, w_cross[h]), down_y)
        send(f"sx{h}", w_at(0, 1, w_cross[h]), sib)

    def t_partner(h):
        got(f"xh{h}")
        send(f"z+1{h}", t_at(0, 1, t_cross[h]), up_z)
        send(f"z-1{h}", t_at(0, 1, t_cross[h]), down_z)

    w_partner("0")
    t_partner("0")
    got("y+01")
    send("s-1", w_at(-1, 0, w_parts[1]), sib)
    got("y-00")
    send("s+0", w_at(1, 0, w_parts[0]), sib)
    got("z+01", "z-00")
    w_partner("1")
    t_partner("1")
    got("fy-0", "fy+0")
    send("xlf", w_at(2, 0, w_far[1]), over_lo)
    got("fz-0")
    send("xhf", t_at(2, 0, t_far[1]), over_hi)
    got("fz+0")
    send("s2", w_at(2, 0, (0, 2 * half)), sib)
    own_w.wait()
    own_t.wait()
    got("s00", "s01", "s-0", "s-1", "s+0", "s+1", "s2")
    multiply(0)
    w_partner("2")
    t_partner("2")
    got("y+10")
    send("fy+1", w_at(-1, 1, w_far[0]), up_y)
    got("z+10")
    send("fz+1", t_at(-1, 1, t_far[0]), up_z)
    send("sx-0", w_at(-1, 1, w_cross["0"]), sib)
    got("y-10")
    send("sx+0", w_at(1, 1, w_cross["0"]), sib)
    got("z-10")
    got("y-11")
    send("fy-1", w_at(1, 1, w_far[2]), down_y)
    got("z-11")
    send("fz-1", t_at(1, 1, t_far[2]), down_z)
    send("sx+1", w_at(1, 1, w_cross["1"]), sib)
    got("sx0", "sx1", "sx2")
    multiply(1)
    got("y+11")
    send("sx-1", w_at(-1, 1, w_cross["1"]), sib)
    got("y+12")
    send("sx-2", w_at(-1, 1, w_cross["2"]), sib)
    got("y-12")
    send("sx+2", w_at(1, 1, w_cross["2"]), sib)
    got("z+11", "z+12", "z-12")
    got("sx-0", "sx-1", "sx-2", "sx+0", "sx+1", "sx+2")
    multiply(2, 0, 4)
    got("fy+1")
    send("sf0", w_at(2, 1, w_far[0]), sib)
    got("xlf")
    send("sf1", w_at(2, 1, w_far[1]), sib)
    got("fy-1")
    send("sf2", w_at(2, 1, w_far[2]), sib)
    got("sf0", "sf1", "sf2")
    multiply_rest(block_at(0)[0])
    got("fz+1", "fz-1", "xhf")

    part = V // 4
    me = row * 16 + col
    row_base = row * acc.shape[0]
    col_base = col * acc.shape[1]

    def exchange(t):
        i, j = block_at(t)

        @pl.when(jnp.logical_and(lax.rem(t, 2) == 0, t >= 2))
        def _():
            multiply_rest(i)

        @pl.when(lax.rem(t, 2) == 0)
        def _():
            add_product(late, i * V, V)

        rows = pl.ds(pl.multiple_of(i * V, V), V)
        cols = pl.ds(pl.multiple_of(j * V, V), V)
        select = pick[...]
        cyc = acc[rows, cols]
        hi = cyc.astype(jnp.bfloat16)
        lo = (cyc - hi.astype(jnp.float32)).astype(jnp.bfloat16)

        def exchanged(piece):
            moved = jnp.dot(select, piece, preferred_element_type=jnp.float32).astype(jnp.bfloat16)
            return lax.dot_general(
                select, moved, (((1,), (1,)), ((), ())), preferred_element_type=jnp.float32
            )

        combined = (2.0 * cyc - (exchanged(hi) + exchanged(lo))).astype(jnp.bfloat16)
        comb[rows, cols] = combined
        comb_t[cols, rows] = combined.T

    def pieces(t, s):
        i, j = block_at(t)
        n = t * 4 + s
        row_src = comb.at[
            pl.ds(pl.multiple_of(i * V + s * part, part), part), pl.ds(pl.multiple_of(j * V, V), V)
        ]
        row_dst = rows_ref.at[:, pl.ds(pl.multiple_of(col_base + j * V, V), V)]
        col_src = comb_t.at[
            pl.ds(pl.multiple_of(j * V + s * part, part), part), pl.ds(pl.multiple_of(i * V, V), V)
        ]
        col_dst = cols_ref.at[:, pl.ds(pl.multiple_of(row_base + i * V, V), V)]
        return (
            (row_src, row_dst, row_sems.at[n], land_sems.at[0], row, i * 4 + s),
            (col_src, col_dst, col_sems.at[n], land_sems.at[1], col // 2, lax.rem(col, 2) * 8 + j * 4 + s),
        )

    def each_piece(t, remote_step, local_step):
        def piece(s, carry):
            for src, dst, sent, landed, to_row, to_col in pieces(t, s):
                here = to_row * 16 + to_col == me

                @pl.when(here)
                def _():
                    local_step(pltpu.make_async_copy(src, dst, landed))

                @pl.when(jnp.logical_not(here))
                def _():
                    remote_step(
                        pltpu.make_async_remote_copy(
                            src_ref=src, dst_ref=dst, send_sem=sent, recv_sem=landed,
                            device_id=(to_row, to_col), device_id_type=MESH,
                        )
                    )

            return carry

        lax.fori_loop(0, 4, piece, 0)

    def start(t):
        each_piece(t, lambda copy: copy.start(), lambda copy: copy.start())

    def step(t, carry):
        exchange(t)
        start(t)
        return carry

    lax.fori_loop(0, 8, step, 0)
    for copy in copies.values():
        copy.wait_send()

    def sent(t, carry):
        each_piece(t, lambda copy: copy.wait_send(), lambda copy: None)
        return carry

    lax.fori_loop(0, 8, sent, 0)
    pltpu.make_async_copy(rows_ref, rows_ref, land_sems.at[0]).wait()
    pltpu.make_async_copy(cols_ref, cols_ref, land_sems.at[1]).wait()


def update_kernel(
    rows_ref, cols_ref, old_ref, virt_ref, occ_ref, out_ref, old, out, virt, occ, in_sems, out_sems
):
    slab_rows = old.shape[0]
    chunks = in_sems.shape[0] - 2
    width = old.shape[1] // chunks
    slab = lax.axis_index("row") * 16 + lax.axis_index("col")
    small = (
        pltpu.make_async_copy(virt_ref, virt, in_sems.at[chunks]),
        pltpu.make_async_copy(occ_ref, occ, in_sems.at[chunks + 1]),
    )
    for copy in small:
        copy.start()

    def chunk_of(n):
        return (slice(None), pl.ds(n * width, width))

    reads = [
        pltpu.make_async_copy(old_ref.at[chunk_of(n)], old.at[chunk_of(n)], in_sems.at[n])
        for n in range(chunks)
    ]
    writes = [
        pltpu.make_async_copy(out.at[chunk_of(n)], out_ref.at[chunk_of(n)], out_sems.at[n])
        for n in range(chunks)
    ]
    for copy in reads:
        copy.start()
    for copy in small:
        copy.wait()
    per_orbital = V // slab_rows
    virtual = virt[...].reshape(1, V)
    lanes = lax.broadcasted_iota(jnp.int32, (slab_rows, V), 1)
    wanted = lax.broadcasted_iota(jnp.int32, (slab_rows, V), 0) + lax.rem(slab, per_orbital) * slab_rows
    row_energy = (
        jnp.sum(jnp.where(lanes == wanted, virtual, 0.0), axis=1, keepdims=True)
        - occ[slab // per_orbital]
    )
    for n in range(chunks):
        reads[n].wait()

        def orbital(j, carry):
            cols = pl.ds(pl.multiple_of(j * V, V), V)
            denominator = row_energy + (virtual - occ[j])
            paired = rows_ref[:, cols].astype(jnp.float32) + cols_ref[:, cols].astype(jnp.float32)
            out[:, cols] = old[:, cols].astype(jnp.float32) + paired / denominator
            return carry

        lax.fori_loop(n * (width // V), (n + 1) * (width // V), orbital, 0)
        writes[n].start()
    for copy in writes:
        copy.wait()


def on_device(interaction, cycle_amps, tile_mask, virt_perm, occ_energy, virt_energy, old_amps):
    row_count, depth = interaction.shape
    out_cols = cycle_amps.shape[1]
    slab_rows, total_cols = old_amps.shape
    rows, cols = pl.pallas_call(
        cycle_kernel,
        name="cycle",
        out_shape=(jax.ShapeDtypeStruct((slab_rows, total_cols), jnp.bfloat16),) * 2,
        in_specs=[pl.BlockSpec(memory_space=pltpu.HBM)] * 4,
        out_specs=(pl.BlockSpec(memory_space=pl.ANY),) * 2,
        scratch_shapes=[
            pltpu.VMEM((8, row_count, 2 * depth), jnp.bfloat16),
            pltpu.VMEM((8, cycle_amps.shape[0], out_cols), jnp.bfloat16),
            pltpu.VMEM((row_count, out_cols), jnp.float32),
            pltpu.VMEM((row_count, out_cols), jnp.bfloat16),
            pltpu.VMEM((out_cols, row_count), jnp.bfloat16),
            pltpu.VMEM((V, V), jnp.bfloat16),
            pltpu.SMEM(tile_mask.shape[::-1], jnp.int32),
            pltpu.VMEM((V,), jnp.int32),
            pltpu.SemaphoreType.DMA((64,)),
            pltpu.SemaphoreType.DMA((64,)),
            pltpu.SemaphoreType.DMA((4,)),
            pltpu.SemaphoreType.DMA((32,)),
            pltpu.SemaphoreType.DMA((32,)),
            pltpu.SemaphoreType.DMA((2,)),
            pltpu.SemaphoreType.REGULAR((6,)),
        ],
        compiler_params=pltpu.CompilerParams(
            collective_id=1, has_side_effects=True, vmem_limit_bytes=44 * 1024 * 1024
        ),
    )(
        *(
            pltpu.with_memory_space_constraint(operand, pltpu.HBM)
            for operand in (tile_mask.T, virt_perm, interaction, cycle_amps)
        )
    )
    chunks = 4
    return pl.pallas_call(
        update_kernel,
        name="update",
        out_shape=jax.ShapeDtypeStruct((slab_rows, total_cols), jnp.float32),
        in_specs=[pl.BlockSpec(memory_space=pltpu.VMEM)] * 2 + [pl.BlockSpec(memory_space=pltpu.HBM)] * 3,
        out_specs=pl.BlockSpec(memory_space=pltpu.HBM),
        scratch_shapes=[
            pltpu.VMEM((slab_rows, total_cols), jnp.bfloat16),
            pltpu.VMEM((slab_rows, total_cols), jnp.float32),
            pltpu.VMEM((V,), jnp.float32),
            pltpu.SMEM((occ_energy.shape[0],), jnp.float32),
            pltpu.SemaphoreType.DMA((chunks + 2,)),
            pltpu.SemaphoreType.DMA((chunks,)),
        ],
        compiler_params=pltpu.CompilerParams(vmem_limit_bytes=12 * 1024 * 1024),
    )(rows, cols, old_amps, virt_energy, occ_energy)


def solution(mesh):
    placed = (P("row", "col"), P("row", "col"), P(), P(), P(), P(), P(("row", "col"), None))
    return jax.shard_map(
        on_device, mesh=mesh, in_specs=placed, out_specs=P(("row", "col"), None), check_vma=False
    )
```

```python
import functools

import jax
import jax.numpy as jnp
from jax import lax
from jax.experimental import pallas as pl
from jax.experimental.pallas import tpu as pltpu
from jax.sharding import PartitionSpec as P

V = 384
TILE = 768
MESH = pl.DeviceIdType.MESH


def place():
    r = lax.axis_index("row")
    c = lax.axis_index("col")
    return r // 2, r % 2, c // 4, (c // 2) % 2, c % 2


def device(z, xh, y, xl, k):
    return (lax.rem(z + 4, 4) * 2 + xh, lax.rem(y + 4, 4) * 4 + xl * 2 + k)


def cycle_kernel(
    mask_ref, perm_ref, w_ref, t_ref,
    rows_ref, cols_ref,
    wb, tb, acc, comb, comb_t, pick, mask, perm, ssem, rsem, lsem, row_sems, col_sems, land_sems, near_sems,
):
    row, col = lax.axis_index("row"), lax.axis_index("col")
    z, xh, y, xl, k = place()
    depth = w_ref.shape[1]
    tiles = acc.shape[0] // TILE
    k_cols = pl.ds(pl.multiple_of(k * depth, 128), depth)

    up_y, down_y = device(z, xh, y + 1, xl, k), device(z, xh, y - 1, xl, k)
    up_z, down_z = device(z + 1, xh, y, xl, k), device(z - 1, xh, y, xl, k)
    over_lo = device(z, xh, y, 1 - xl, k)
    over_hi = device(z, 1 - xh, y, xl, k)
    sib = device(z, xh, y, xl, 1 - k)

    barrier = pltpu.get_barrier_semaphore()

    peers = (up_y, down_y, up_z, down_z, over_lo, over_hi, sib)
    for peer in peers:
        pl.semaphore_signal(barrier, inc=1, device_id=peer, device_id_type=MESH)

    def slot(along, which):
        return lax.rem(along + 4, 4) * 2 + which

    half = wb.shape[1] // 2
    w_parts = ((0, half), (half, half))
    t_parts = ((0, V), (V, V))
    w_far = ((0, 336), (672, 864), (336, 336))
    t_far = ((0, 288), (576, 192), (288, 288))
    w_cross = {"0": (0, half), "1": (half, half // 2), "2": (3 * half // 2, half // 2)}
    t_cross = {"0": (0, V), "1": (V, V // 2), "2": (3 * V // 2, V // 2)}

    def w_at(dy, e, part):
        return wb.at[slot(y + dy, xl if e == 0 else 1 - xl), pl.ds(*part), k_cols]

    def t_at(dz, e, part):
        return tb.at[slot(z + dz, xh if e == 0 else 1 - xh), pl.ds(*part), :]

    copies = {}

    def send(name, ref, peer, src=None):
        i = len(copies)
        copies[name] = pltpu.make_async_remote_copy(
            src_ref=ref if src is None else src,
            dst_ref=ref,
            send_sem=ssem.at[i],
            recv_sem=rsem.at[i],
            device_id=peer,
            device_id_type=MESH,
        )
        copies[name].start()

    def got(*names):
        for name in names:
            copies[name].wait_recv()

    own_w = pltpu.make_async_copy(w_ref, wb.at[slot(y, xl), :, k_cols], lsem.at[0])
    own_t = pltpu.make_async_copy(t_ref, tb.at[slot(z, xh)], lsem.at[1])
    small = (
        pltpu.make_async_copy(mask_ref, mask, lsem.at[2]),
        pltpu.make_async_copy(perm_ref, perm, lsem.at[3]),
    )
    for copy in (*small, own_w, own_t):
        copy.start()
    pl.semaphore_wait(barrier, len(peers))

    for first in (0, 1):
        a, b = first, 1 - first
        w_a, w_b, t_a, t_b = w_parts[a], w_parts[b], t_parts[a], t_parts[b]
        send(f"y+0{a}", w_at(0, 0, w_a), up_y, w_ref.at[pl.ds(*w_a), :])
        send(f"y-0{b}", w_at(0, 0, w_b), down_y, w_ref.at[pl.ds(*w_b), :])
        send(f"z+0{a}", t_at(0, 0, t_a), up_z, t_ref.at[pl.ds(*t_a), :])
        send(f"z-0{b}", t_at(0, 0, t_b), down_z, t_ref.at[pl.ds(*t_b), :])
        for h in ("0",) if first == 0 else ("1", "2"):
            w_h, t_h = w_cross[h], t_cross[h]
            send(f"xl{h}", w_at(0, 0, w_h), over_lo, w_ref.at[pl.ds(*w_h), :])
            send(f"xh{h}", t_at(0, 0, t_h), over_hi, t_ref.at[pl.ds(*t_h), :])
        send(f"s0{a}", w_at(0, 0, w_a), sib, w_ref.at[pl.ds(*w_a), :])

    acc[...] = jnp.zeros_like(acc)
    for copy in small:
        copy.wait()
    orbital = lax.broadcasted_iota(jnp.int32, pick.shape, 0)
    pick[...] = jnp.where(orbital == perm[...].reshape(1, V), 1.0, 0.0).T.astype(jnp.bfloat16)

    def class_of(distance, other):
        near = lax.rem(distance + 8, 4)
        ring = jnp.where(near == 0, 1, jnp.where(near == 2, 3, 2))
        return jnp.where(other == 0, 0, ring)

    def farness(q):
        return jnp.maximum(
            class_of(q // 2 - y, lax.rem(q % 2 + xl, 2)),
            class_of(q // 2 - z, lax.rem(q % 2 + xh, 2)),
        )

    def add_product(q, start, size):
        at = pl.ds(pl.multiple_of(start, size), size)
        kept = mask[q, row * tiles + start // TILE].astype(jnp.float32)
        acc[at, :] += kept * jnp.dot(wb[q, at, :], tb[q], preferred_element_type=jnp.float32)

    def multiply(stage, begin=0, end=8):
        def block(q, carry):
            @pl.when(farness(q) == stage)
            def _():
                def tile(p, inner):
                    add_product(q, p * TILE, TILE)
                    return inner

                lax.fori_loop(0, tiles, tile, 0)

            return carry

        lax.fori_loop(begin, end, block, 0)

    def block_at(t):
        n = t // 4 * 2 + lax.rem(t, 2)
        hop = jnp.where(n == 0, 1, jnp.where(n == 1, 3, jnp.where(n == 2, 2, 0)))
        return lax.rem(y + jnp.where(k == 0, hop, 4 - hop), 4), lax.rem(t // 2 + t + 1 + y, 2)

    late = slot(z + 2, 1 - xh)

    def multiply_rest(i):
        def block(q, carry):
            far = farness(q)
            left = jnp.logical_or(far == 3, jnp.logical_and(far == 2, q >= 4))

            @pl.when(jnp.logical_and(left, q != late))
            def _():
                add_product(q, i * V, V)

            return carry

        lax.fori_loop(0, 8, block, 0)

    def spread(n, carry):
        for peer in peers:
            pl.semaphore_signal(near_sems.at[n], inc=1, device_id=peer, device_id_type=MESH)
        pl.semaphore_wait(near_sems.at[n], len(peers))
        return carry

    lax.fori_loop(0, 6, spread, 0)

    got("y+00")
    send("fy+0", w_at(-1, 0, w_parts[0]), up_y)
    got("z+00")
    send("fz+0", t_at(-1, 0, t_parts[0]), up_z)
    got("y-01")
    send("fy-0", w_at(1, 0, w_parts[1]), down_y)
    got("z-01")
    send("fz-0", t_at(1, 0, t_parts[1]), down_z)
    send("s-0", w_at(-1, 0, w_parts[0]), sib)
    send("s+1", w_at(1, 0, w_parts[1]), sib)

    def w_partner(h):
        got(f"xl{h}")
        send(f"y+1{h}", w_at(0, 1, w_cross[h]), up_y)
        send(f"y-1{h}", w_at(0, 1, w_cross[h]), down_y)
        send(f"sx{h}", w_at(0, 1, w_cross[h]), sib)

    def t_partner(h):
        got(f"xh{h}")
        send(f"z+1{h}", t_at(0, 1, t_cross[h]), up_z)
        send(f"z-1{h}", t_at(0, 1, t_cross[h]), down_z)

    w_partner("0")
    t_partner("0")
    got("y+01")
    send("s-1", w_at(-1, 0, w_parts[1]), sib)
    got("y-00")
    send("s+0", w_at(1, 0, w_parts[0]), sib)
    got("z+01", "z-00")
    w_partner("1")
    t_partner("1")
    got("fy-0", "fy+0")
    send("xlf", w_at(2, 0, w_far[1]), over_lo)
    got("fz-0")
    send("xhf", t_at(2, 0, t_far[1]), over_hi)
    got("fz+0")
    send("s2", w_at(2, 0, (0, 2 * half)), sib)
    own_w.wait()
    own_t.wait()
    got("s00", "s01", "s-0", "s-1", "s+0", "s+1", "s2")
    multiply(0)
    w_partner("2")
    t_partner("2")
    got("y+10")
    send("fy+1", w_at(-1, 1, w_far[0]), up_y)
    got("z+10")
    send("fz+1", t_at(-1, 1, t_far[0]), up_z)
    send("sx-0", w_at(-1, 1, w_cross["0"]), sib)
    got("y-10")
    send("sx+0", w_at(1, 1, w_cross["0"]), sib)
    got("z-10")
    got("y-11")
    send("fy-1", w_at(1, 1, w_far[2]), down_y)
    got("z-11")
    send("fz-1", t_at(1, 1, t_far[2]), down_z)
    send("sx+1", w_at(1, 1, w_cross["1"]), sib)
    got("sx0", "sx1", "sx2")
    multiply(1)
    got("y+11")
    send("sx-1", w_at(-1, 1, w_cross["1"]), sib)
    got("y+12")
    send("sx-2", w_at(-1, 1, w_cross["2"]), sib)
    got("y-12")
    send("sx+2", w_at(1, 1, w_cross["2"]), sib)
    got("z+11", "z+12", "z-12")
    got("sx-0", "sx-1", "sx-2", "sx+0", "sx+1", "sx+2")
    multiply(2, 0, 4)
    got("fy+1")
    send("sf0", w_at(2, 1, w_far[0]), sib)
    got("xlf")
    send("sf1", w_at(2, 1, w_far[1]), sib)
    got("fy-1")
    send("sf2", w_at(2, 1, w_far[2]), sib)
    got("sf0", "sf1", "sf2")
    multiply_rest(block_at(0)[0])
    got("fz+1", "fz-1", "xhf")

    part = V // 4
    me = row * 16 + col
    row_base = row * acc.shape[0]
    col_base = col * acc.shape[1]

    def exchange(t):
        i, j = block_at(t)

        fresh = lax.rem(t // 2, 2) == 0

        @pl.when(jnp.logical_and(fresh, t > 0))
        def _():
            multiply_rest(i)

        @pl.when(fresh)
        def _():
            add_product(late, i * V, V)

        rows = pl.ds(pl.multiple_of(i * V, V), V)
        cols = pl.ds(pl.multiple_of(j * V, V), V)
        select = pick[...]
        cyc = acc[rows, cols]
        hi = cyc.astype(jnp.bfloat16)
        lo = (cyc - hi.astype(jnp.float32)).astype(jnp.bfloat16)

        def exchanged(piece):
            moved = jnp.dot(select, piece, preferred_element_type=jnp.float32).astype(jnp.bfloat16)
            return lax.dot_general(
                select, moved, (((1,), (1,)), ((), ())), preferred_element_type=jnp.float32
            )

        combined = (2.0 * cyc - (exchanged(hi) + exchanged(lo))).astype(jnp.bfloat16)
        comb[rows, cols] = combined
        comb_t[cols, rows] = combined.T

    def pieces(t, s):
        i, j = block_at(t)
        n = t * 4 + s
        row_src = comb.at[
            pl.ds(pl.multiple_of(i * V + s * part, part), part), pl.ds(pl.multiple_of(j * V, V), V)
        ]
        row_dst = rows_ref.at[:, pl.ds(pl.multiple_of(col_base + j * V, V), V)]
        col_src = comb_t.at[
            pl.ds(pl.multiple_of(j * V + s * part, part), part), pl.ds(pl.multiple_of(i * V, V), V)
        ]
        col_dst = cols_ref.at[:, pl.ds(pl.multiple_of(row_base + i * V, V), V)]
        return (
            (row_src, row_dst, row_sems.at[n], land_sems.at[0], row, i * 4 + s),
            (col_src, col_dst, col_sems.at[n], land_sems.at[1], col // 2, lax.rem(col, 2) * 8 + j * 4 + s),
        )

    def each_piece(t, remote_step, local_step):
        def piece(s, carry):
            for src, dst, sent, landed, to_row, to_col in pieces(t, s):
                here = to_row * 16 + to_col == me

                @pl.when(here)
                def _():
                    local_step(pltpu.make_async_copy(src, dst, landed))

                @pl.when(jnp.logical_not(here))
                def _():
                    remote_step(
                        pltpu.make_async_remote_copy(
                            src_ref=src, dst_ref=dst, send_sem=sent, recv_sem=landed,
                            device_id=(to_row, to_col), device_id_type=MESH,
                        )
                    )

            return carry

        lax.fori_loop(0, 4, piece, 0)

    def start(t):
        each_piece(t, lambda copy: copy.start(), lambda copy: copy.start())

    def step(t, carry):
        exchange(t)
        start(t)
        return carry

    lax.fori_loop(0, 8, step, 0)
    for copy in copies.values():
        copy.wait_send()

    def sent(t, carry):
        each_piece(t, lambda copy: copy.wait_send(), lambda copy: None)
        return carry

    lax.fori_loop(0, 8, sent, 0)
    pltpu.make_async_copy(rows_ref, rows_ref, land_sems.at[0]).wait()
    pltpu.make_async_copy(cols_ref, cols_ref, land_sems.at[1]).wait()


def update_kernel(rows_ref, cols_ref, old_ref, virt_ref, occ_ref, out_ref, out, occ, in_sem, out_sems):
    slab_rows, total_cols = old_ref.shape
    chunks = out_sems.shape[0]
    width = total_cols // chunks
    slab = lax.axis_index("row") * 16 + lax.axis_index("col")
    energies = pltpu.make_async_copy(occ_ref, occ, in_sem.at[0])
    energies.start()

    def chunk_of(n):
        return (slice(None), pl.ds(n * width, width))

    writes = [
        pltpu.make_async_copy(out.at[chunk_of(n)], out_ref.at[chunk_of(n)], out_sems.at[n])
        for n in range(chunks)
    ]
    per_orbital = V // slab_rows
    virtual = virt_ref[...].reshape(1, V)
    lanes = lax.broadcasted_iota(jnp.int32, (slab_rows, V), 1)
    wanted = lax.broadcasted_iota(jnp.int32, (slab_rows, V), 0) + lax.rem(slab, per_orbital) * slab_rows
    row_energy = jnp.sum(jnp.where(lanes == wanted, virtual, 0.0), axis=1, keepdims=True)
    energies.wait()
    row_energy = row_energy - occ[slab // per_orbital]
    for n in range(chunks):

        def orbital(j, carry):
            cols = pl.ds(pl.multiple_of(j * V, V), V)
            denominator = row_energy + (virtual - occ[j])
            paired = rows_ref[:, cols].astype(jnp.float32) + cols_ref[:, cols].astype(jnp.float32)
            out[:, cols] = old_ref[:, cols].astype(jnp.float32) + paired / denominator
            return carry

        lax.fori_loop(n * (width // V), (n + 1) * (width // V), orbital, 0)
        writes[n].start()
    for copy in writes:
        copy.wait()


def on_device(interaction, cycle_amps, tile_mask, virt_perm, occ_energy, virt_energy, old_amps):
    row_count, depth = interaction.shape
    out_cols = cycle_amps.shape[1]
    slab_rows, total_cols = old_amps.shape
    rows, cols = pl.pallas_call(
        cycle_kernel,
        name="cycle",
        out_shape=(jax.ShapeDtypeStruct((slab_rows, total_cols), jnp.bfloat16),) * 2,
        in_specs=[pl.BlockSpec(memory_space=pltpu.HBM)] * 4,
        out_specs=(pl.BlockSpec(memory_space=pl.ANY),) * 2,
        scratch_shapes=[
            pltpu.VMEM((8, row_count, 2 * depth), jnp.bfloat16),
            pltpu.VMEM((8, cycle_amps.shape[0], out_cols), jnp.bfloat16),
            pltpu.VMEM((row_count, out_cols), jnp.float32),
            pltpu.VMEM((row_count, out_cols), jnp.bfloat16),
            pltpu.VMEM((out_cols, row_count), jnp.bfloat16),
            pltpu.VMEM((V, V), jnp.bfloat16),
            pltpu.SMEM(tile_mask.shape[::-1], jnp.int32),
            pltpu.VMEM((V,), jnp.int32),
            pltpu.SemaphoreType.DMA((64,)),
            pltpu.SemaphoreType.DMA((64,)),
            pltpu.SemaphoreType.DMA((4,)),
            pltpu.SemaphoreType.DMA((32,)),
            pltpu.SemaphoreType.DMA((32,)),
            pltpu.SemaphoreType.DMA((2,)),
            pltpu.SemaphoreType.REGULAR((6,)),
        ],
        compiler_params=pltpu.CompilerParams(
            collective_id=1, has_side_effects=True, vmem_limit_bytes=44 * 1024 * 1024
        ),
    )(
        *(
            pltpu.with_memory_space_constraint(operand, pltpu.HBM)
            for operand in (tile_mask.T, virt_perm, interaction, cycle_amps)
        )
    )
    chunks = 8
    return pl.pallas_call(
        update_kernel,
        name="update",
        out_shape=jax.ShapeDtypeStruct((slab_rows, total_cols), jnp.float32),
        in_specs=[pl.BlockSpec(memory_space=pltpu.VMEM)] * 4 + [pl.BlockSpec(memory_space=pltpu.HBM)],
        out_specs=pl.BlockSpec(memory_space=pltpu.HBM),
        scratch_shapes=[
            pltpu.VMEM((slab_rows, total_cols), jnp.float32),
            pltpu.SMEM((occ_energy.shape[0],), jnp.float32),
            pltpu.SemaphoreType.DMA((1,)),
            pltpu.SemaphoreType.DMA((chunks,)),
        ],
        compiler_params=pltpu.CompilerParams(vmem_limit_bytes=12 * 1024 * 1024),
    )(rows, cols, old_amps, virt_energy, occ_energy)


def solution(mesh):
    placed = (P("row", "col"), P("row", "col"), P(), P(), P(), P(), P(("row", "col"), None))
    return jax.shard_map(
        on_device, mesh=mesh, in_specs=placed, out_specs=P(("row", "col"), None), check_vma=False
    )
```

```python
import functools

import jax
import jax.numpy as jnp
from jax import lax
from jax.experimental import pallas as pl
from jax.experimental.pallas import tpu as pltpu
from jax.sharding import PartitionSpec as P

V = 384
TILE = 768
MESH = pl.DeviceIdType.MESH


def place():
    r = lax.axis_index("row")
    c = lax.axis_index("col")
    return r // 2, r % 2, c // 4, (c // 2) % 2, c % 2


def device(z, xh, y, xl, k):
    return (lax.rem(z + 4, 4) * 2 + xh, lax.rem(y + 4, 4) * 4 + xl * 2 + k)


def cycle_kernel(
    mask_ref, perm_ref, w_ref, t_ref,
    rows_ref, cols_ref,
    wb, tb, acc, comb, comb_t, pick, mask, perm, ssem, rsem, lsem, row_sems, col_sems, land_sems, near_sems,
):
    row, col = lax.axis_index("row"), lax.axis_index("col")
    z, xh, y, xl, k = place()
    depth = w_ref.shape[1]
    tiles = acc.shape[0] // TILE
    k_cols = pl.ds(pl.multiple_of(k * depth, 128), depth)

    up_y, down_y = device(z, xh, y + 1, xl, k), device(z, xh, y - 1, xl, k)
    up_z, down_z = device(z + 1, xh, y, xl, k), device(z - 1, xh, y, xl, k)
    over_lo = device(z, xh, y, 1 - xl, k)
    over_hi = device(z, 1 - xh, y, xl, k)
    sib = device(z, xh, y, xl, 1 - k)

    barrier = pltpu.get_barrier_semaphore()

    peers = (up_y, down_y, up_z, down_z, over_lo, over_hi, sib)
    for peer in peers:
        pl.semaphore_signal(barrier, inc=1, device_id=peer, device_id_type=MESH)

    def slot(along, which):
        return lax.rem(along + 4, 4) * 2 + which

    half = wb.shape[1] // 2
    w_parts = ((0, half), (half, half))
    t_parts = ((0, V), (V, V))
    w_far = ((0, 336), (672, 864), (336, 336))
    t_far = ((0, 288), (576, 192), (288, 288))
    w_cross = {"0": (0, half), "1": (half, half // 2), "2": (3 * half // 2, half // 2)}
    t_cross = {"0": (0, V), "1": (V, V // 2), "2": (3 * V // 2, V // 2)}

    def w_at(dy, e, part):
        return wb.at[slot(y + dy, xl if e == 0 else 1 - xl), pl.ds(*part), k_cols]

    def t_at(dz, e, part):
        return tb.at[slot(z + dz, xh if e == 0 else 1 - xh), pl.ds(*part), :]

    copies = {}

    def send(name, ref, peer, src=None):
        i = len(copies)
        copies[name] = pltpu.make_async_remote_copy(
            src_ref=ref if src is None else src,
            dst_ref=ref,
            send_sem=ssem.at[i],
            recv_sem=rsem.at[i],
            device_id=peer,
            device_id_type=MESH,
        )
        copies[name].start()

    def got(*names):
        for name in names:
            copies[name].wait_recv()

    own_w = pltpu.make_async_copy(w_ref, wb.at[slot(y, xl), :, k_cols], lsem.at[0])
    own_t = pltpu.make_async_copy(t_ref, tb.at[slot(z, xh)], lsem.at[1])
    small = (
        pltpu.make_async_copy(mask_ref, mask, lsem.at[2]),
        pltpu.make_async_copy(perm_ref, perm, lsem.at[3]),
    )
    for copy in (*small, own_w, own_t):
        copy.start()
    pl.semaphore_wait(barrier, len(peers))

    for first in (0, 1):
        a, b = first, 1 - first
        w_a, w_b, t_a, t_b = w_parts[a], w_parts[b], t_parts[a], t_parts[b]
        send(f"y+0{a}", w_at(0, 0, w_a), up_y, w_ref.at[pl.ds(*w_a), :])
        send(f"y-0{b}", w_at(0, 0, w_b), down_y, w_ref.at[pl.ds(*w_b), :])
        send(f"z+0{a}", t_at(0, 0, t_a), up_z, t_ref.at[pl.ds(*t_a), :])
        send(f"z-0{b}", t_at(0, 0, t_b), down_z, t_ref.at[pl.ds(*t_b), :])
        for h in ("0",) if first == 0 else ("1", "2"):
            w_h, t_h = w_cross[h], t_cross[h]
            send(f"xl{h}", w_at(0, 0, w_h), over_lo, w_ref.at[pl.ds(*w_h), :])
            send(f"xh{h}", t_at(0, 0, t_h), over_hi, t_ref.at[pl.ds(*t_h), :])
        send(f"s0{a}", w_at(0, 0, w_a), sib, w_ref.at[pl.ds(*w_a), :])

    acc[...] = jnp.zeros_like(acc)
    for copy in small:
        copy.wait()
    orbital = lax.broadcasted_iota(jnp.int32, pick.shape, 0)
    pick[...] = jnp.where(orbital == perm[...].reshape(1, V), 1.0, 0.0).T.astype(jnp.bfloat16)

    def class_of(distance, other):
        near = lax.rem(distance + 8, 4)
        ring = jnp.where(near == 0, 1, jnp.where(near == 2, 3, 2))
        return jnp.where(other == 0, 0, ring)

    def farness(q):
        return jnp.maximum(
            class_of(q // 2 - y, lax.rem(q % 2 + xl, 2)),
            class_of(q // 2 - z, lax.rem(q % 2 + xh, 2)),
        )

    def add_product(q, start, size):
        at = pl.ds(pl.multiple_of(start, size), size)
        kept = mask[q, row * tiles + start // TILE].astype(jnp.float32)
        acc[at, :] += kept * jnp.dot(wb[q, at, :], tb[q], preferred_element_type=jnp.float32)

    def multiply(stage, begin=0, end=8):
        def block(q, carry):
            @pl.when(farness(q) == stage)
            def _():
                def tile(p, inner):
                    add_product(q, p * TILE, TILE)
                    return inner

                lax.fori_loop(0, tiles, tile, 0)

            return carry

        lax.fori_loop(begin, end, block, 0)

    def block_at(t):
        n = t // 4 * 2 + lax.rem(t, 2)
        hop = jnp.where(n == 0, 1, jnp.where(n == 1, 3, jnp.where(n == 2, 2, 0)))
        return lax.rem(y + jnp.where(k == 0, hop, 4 - hop), 4), lax.rem(t // 2 + t + 1 + y, 2)

    late = slot(z + 2, 1 - xh)

    def multiply_rest(i):
        def block(q, carry):
            far = farness(q)
            left = jnp.logical_or(far == 3, jnp.logical_and(far == 2, q >= 4))

            @pl.when(jnp.logical_and(left, q != late))
            def _():
                add_product(q, i * V, V)

            return carry

        lax.fori_loop(0, 8, block, 0)

    def spread(n, carry):
        for peer in peers:
            pl.semaphore_signal(near_sems.at[n], inc=1, device_id=peer, device_id_type=MESH)
        pl.semaphore_wait(near_sems.at[n], len(peers))
        return carry

    lax.fori_loop(0, 6, spread, 0)

    got("y+00")
    send("fy+0", w_at(-1, 0, w_parts[0]), up_y)
    got("z+00")
    send("fz+0", t_at(-1, 0, t_parts[0]), up_z)
    got("y-01")
    send("fy-0", w_at(1, 0, w_parts[1]), down_y)
    got("z-01")
    send("fz-0", t_at(1, 0, t_parts[1]), down_z)
    send("s-0", w_at(-1, 0, w_parts[0]), sib)
    send("s+1", w_at(1, 0, w_parts[1]), sib)

    def w_partner(h):
        got(f"xl{h}")
        send(f"y+1{h}", w_at(0, 1, w_cross[h]), up_y)
        send(f"y-1{h}", w_at(0, 1, w_cross[h]), down_y)
        send(f"sx{h}", w_at(0, 1, w_cross[h]), sib)

    def t_partner(h):
        got(f"xh{h}")
        send(f"z+1{h}", t_at(0, 1, t_cross[h]), up_z)
        send(f"z-1{h}", t_at(0, 1, t_cross[h]), down_z)

    w_partner("0")
    t_partner("0")
    got("y+01")
    send("s-1", w_at(-1, 0, w_parts[1]), sib)
    got("y-00")
    send("s+0", w_at(1, 0, w_parts[0]), sib)
    got("z+01", "z-00")
    w_partner("1")
    t_partner("1")
    got("fy-0", "fy+0")
    send("xlf", w_at(2, 0, w_far[1]), over_lo)
    got("fz-0")
    send("xhf", t_at(2, 0, t_far[1]), over_hi)
    got("fz+0")
    send("s2", w_at(2, 0, (0, 2 * half)), sib)
    own_w.wait()
    own_t.wait()
    got("s00", "s01", "s-0", "s-1", "s+0", "s+1", "s2")
    multiply(0)
    w_partner("2")
    t_partner("2")
    got("y+10")
    send("fy+1", w_at(-1, 1, w_far[0]), up_y)
    got("z+10")
    send("fz+1", t_at(-1, 1, t_far[0]), up_z)
    send("sx-0", w_at(-1, 1, w_cross["0"]), sib)
    got("y-10")
    send("sx+0", w_at(1, 1, w_cross["0"]), sib)
    got("z-10")
    got("y-11")
    send("fy-1", w_at(1, 1, w_far[2]), down_y)
    got("z-11")
    send("fz-1", t_at(1, 1, t_far[2]), down_z)
    send("sx+1", w_at(1, 1, w_cross["1"]), sib)
    got("sx0", "sx1", "sx2")
    multiply(1)
    got("y+11")
    send("sx-1", w_at(-1, 1, w_cross["1"]), sib)
    got("y+12")
    send("sx-2", w_at(-1, 1, w_cross["2"]), sib)
    got("y-12")
    send("sx+2", w_at(1, 1, w_cross["2"]), sib)
    got("z+11", "z+12", "z-12")
    got("sx-0", "sx-1", "sx-2", "sx+0", "sx+1", "sx+2")
    multiply(2, 0, 4)
    got("fy+1")
    send("sf0", w_at(2, 1, w_far[0]), sib)
    got("xlf")
    send("sf1", w_at(2, 1, w_far[1]), sib)
    got("fy-1")
    send("sf2", w_at(2, 1, w_far[2]), sib)
    got("sf0", "sf1", "sf2")
    multiply_rest(block_at(0)[0])
    got("fz+1", "fz-1", "xhf")

    part = V // 4
    me = row * 16 + col
    row_base = row * acc.shape[0]
    col_base = col * acc.shape[1]

    def exchange(t):
        i, j = block_at(t)

        fresh = lax.rem(t // 2, 2) == 0

        @pl.when(jnp.logical_and(fresh, t > 0))
        def _():
            multiply_rest(i)

        @pl.when(fresh)
        def _():
            add_product(late, i * V, V)

        rows = pl.ds(pl.multiple_of(i * V, V), V)
        cols = pl.ds(pl.multiple_of(j * V, V), V)
        select = pick[...]
        cyc = acc[rows, cols]
        hi = cyc.astype(jnp.bfloat16)
        lo = (cyc - hi.astype(jnp.float32)).astype(jnp.bfloat16)

        def exchanged(piece):
            moved = jnp.dot(select, piece, preferred_element_type=jnp.float32).astype(jnp.bfloat16)
            return lax.dot_general(
                select, moved, (((1,), (1,)), ((), ())), preferred_element_type=jnp.float32
            )

        combined = (2.0 * cyc - (exchanged(hi) + exchanged(lo))).astype(jnp.bfloat16)
        comb[rows, cols] = combined
        comb_t[cols, rows] = combined.T

    def pieces(t, s):
        i, j = block_at(t)
        n = t * 4 + s
        row_src = comb.at[
            pl.ds(pl.multiple_of(i * V + s * part, part), part), pl.ds(pl.multiple_of(j * V, V), V)
        ]
        row_dst = rows_ref.at[:, pl.ds(pl.multiple_of(col_base + j * V, V), V)]
        col_src = comb_t.at[
            pl.ds(pl.multiple_of(j * V + s * part, part), part), pl.ds(pl.multiple_of(i * V, V), V)
        ]
        col_dst = cols_ref.at[:, pl.ds(pl.multiple_of(row_base + i * V, V), V)]
        return (
            (row_src, row_dst, row_sems.at[n], land_sems.at[0], row, i * 4 + s),
            (col_src, col_dst, col_sems.at[n], land_sems.at[1], col // 2, lax.rem(col, 2) * 8 + j * 4 + s),
        )

    def each_piece(t, remote_step, local_step):
        def piece(s, carry):
            for src, dst, sent, landed, to_row, to_col in pieces(t, s)[::-1]:
                here = to_row * 16 + to_col == me

                @pl.when(here)
                def _():
                    local_step(pltpu.make_async_copy(src, dst, landed))

                @pl.when(jnp.logical_not(here))
                def _():
                    remote_step(
                        pltpu.make_async_remote_copy(
                            src_ref=src, dst_ref=dst, send_sem=sent, recv_sem=landed,
                            device_id=(to_row, to_col), device_id_type=MESH,
                        )
                    )

            return carry

        lax.fori_loop(0, 4, piece, 0)

    def start(t):
        each_piece(t, lambda copy: copy.start(), lambda copy: copy.start())

    def step(t, carry):
        exchange(t)
        start(t)
        return carry

    lax.fori_loop(0, 8, step, 0)
    for copy in copies.values():
        copy.wait_send()

    def sent(t, carry):
        each_piece(t, lambda copy: copy.wait_send(), lambda copy: None)
        return carry

    lax.fori_loop(0, 8, sent, 0)
    pltpu.make_async_copy(rows_ref, rows_ref, land_sems.at[0]).wait()
    pltpu.make_async_copy(cols_ref, cols_ref, land_sems.at[1]).wait()


def update_kernel(rows_ref, cols_ref, old_ref, virt_ref, occ_ref, out_ref, out, occ, in_sem, out_sems):
    slab_rows, total_cols = old_ref.shape
    chunks = out_sems.shape[0]
    width = total_cols // chunks
    slab = lax.axis_index("row") * 16 + lax.axis_index("col")
    energies = pltpu.make_async_copy(occ_ref, occ, in_sem.at[0])
    energies.start()

    def chunk_of(n):
        return (slice(None), pl.ds(n * width, width))

    writes = [
        pltpu.make_async_copy(out.at[chunk_of(n)], out_ref.at[chunk_of(n)], out_sems.at[n])
        for n in range(chunks)
    ]
    per_orbital = V // slab_rows
    virtual = virt_ref[...].reshape(1, V)
    lanes = lax.broadcasted_iota(jnp.int32, (slab_rows, V), 1)
    wanted = lax.broadcasted_iota(jnp.int32, (slab_rows, V), 0) + lax.rem(slab, per_orbital) * slab_rows
    row_energy = jnp.sum(jnp.where(lanes == wanted, virtual, 0.0), axis=1, keepdims=True)
    energies.wait()
    row_energy = row_energy - occ[slab // per_orbital]
    for n in range(chunks):

        def orbital(j, carry):
            cols = pl.ds(pl.multiple_of(j * V, V), V)
            denominator = row_energy + (virtual - occ[j])
            paired = rows_ref[:, cols].astype(jnp.float32) + cols_ref[:, cols].astype(jnp.float32)
            out[:, cols] = old_ref[:, cols].astype(jnp.float32) + paired / denominator
            return carry

        lax.fori_loop(n * (width // V), (n + 1) * (width // V), orbital, 0)
        writes[n].start()
    for copy in writes:
        copy.wait()


def on_device(interaction, cycle_amps, tile_mask, virt_perm, occ_energy, virt_energy, old_amps):
    row_count, depth = interaction.shape
    out_cols = cycle_amps.shape[1]
    slab_rows, total_cols = old_amps.shape
    rows, cols = pl.pallas_call(
        cycle_kernel,
        name="cycle",
        out_shape=(jax.ShapeDtypeStruct((slab_rows, total_cols), jnp.bfloat16),) * 2,
        in_specs=[pl.BlockSpec(memory_space=pltpu.HBM)] * 4,
        out_specs=(pl.BlockSpec(memory_space=pl.ANY),) * 2,
        scratch_shapes=[
            pltpu.VMEM((8, row_count, 2 * depth), jnp.bfloat16),
            pltpu.VMEM((8, cycle_amps.shape[0], out_cols), jnp.bfloat16),
            pltpu.VMEM((row_count, out_cols), jnp.float32),
            pltpu.VMEM((row_count, out_cols), jnp.bfloat16),
            pltpu.VMEM((out_cols, row_count), jnp.bfloat16),
            pltpu.VMEM((V, V), jnp.bfloat16),
            pltpu.SMEM(tile_mask.shape[::-1], jnp.int32),
            pltpu.VMEM((V,), jnp.int32),
            pltpu.SemaphoreType.DMA((64,)),
            pltpu.SemaphoreType.DMA((64,)),
            pltpu.SemaphoreType.DMA((4,)),
            pltpu.SemaphoreType.DMA((32,)),
            pltpu.SemaphoreType.DMA((32,)),
            pltpu.SemaphoreType.DMA((2,)),
            pltpu.SemaphoreType.REGULAR((6,)),
        ],
        compiler_params=pltpu.CompilerParams(
            collective_id=1, has_side_effects=True, vmem_limit_bytes=44 * 1024 * 1024
        ),
    )(
        *(
            pltpu.with_memory_space_constraint(operand, pltpu.HBM)
            for operand in (tile_mask.T, virt_perm, interaction, cycle_amps)
        )
    )
    chunks = 8
    return pl.pallas_call(
        update_kernel,
        name="update",
        out_shape=jax.ShapeDtypeStruct((slab_rows, total_cols), jnp.float32),
        in_specs=[pl.BlockSpec(memory_space=pltpu.VMEM)] * 4 + [pl.BlockSpec(memory_space=pltpu.HBM)],
        out_specs=pl.BlockSpec(memory_space=pltpu.HBM),
        scratch_shapes=[
            pltpu.VMEM((slab_rows, total_cols), jnp.float32),
            pltpu.SMEM((occ_energy.shape[0],), jnp.float32),
            pltpu.SemaphoreType.DMA((1,)),
            pltpu.SemaphoreType.DMA((chunks,)),
        ],
        compiler_params=pltpu.CompilerParams(vmem_limit_bytes=12 * 1024 * 1024),
    )(rows, cols, old_amps, virt_energy, occ_energy)


def solution(mesh):
    placed = (P("row", "col"), P("row", "col"), P(), P(), P(), P(), P(("row", "col"), None))
    return jax.shard_map(
        on_device, mesh=mesh, in_specs=placed, out_specs=P(("row", "col"), None), check_vma=False
    )
```
